128 devices in a mesh: seq: 64 (over y, z, x), head: 2 (over core).
Axes of the slice: x: 4, y: 4, z: 4, core: 2. Of those that a mesh axis runs over, the one named last changes fastest.
Arguments:
- queries: bfloat16 [32768, 2048], P('seq', 'head'), may hold values from -60 to 60
- keys: bfloat16 [32768, 2048], P('seq', 'head'), may hold values from -6 to 6
- values: bfloat16 [32768, 2048], P('seq', 'head'), may hold values from -6 to 6
- out_grad: bfloat16 [32768, 2048], P('seq', 'head'), may hold values from -6 to 6
- rand_ids: int32 [16, 256, 3], replicated, may hold values from 0 to 255, as said below
- glob_ids: int32 [2], replicated, may hold values from 0 to 255, as said below
Outputs:
- out: bfloat16 [32768, 2048], P('seq', 'head')
- query_gradient: bfloat16 [32768, 2048], P('seq', 'head')
- key_grad: bfloat16 [32768, 2048], P('seq', 'head')
- value_grad: bfloat16 [32768, 2048], P('seq', 'head')
The draws below stay inside these ranges and needn't reach their ends.
Inputs may be any that keep to these rules, and one draw needn't show every extreme that they name: `rand_ids`: group the heads into runs of 8 and the query blocks into runs of 4; within one head run and one query run, the entries name key blocks of any one aligned run of 4 blocks (blocks 4j to 4j + 3, those of one index of seq) at most 2 times, and exactly 2 times for some such run. `glob_ids`: the ids are distinct, and one of them is the last block, 255.
All inputs are finite; a program needn't handle non-finite values.
Results may differ from the reference program's by a relative error of at most 0.014.
Values may be sent and summed in bfloat16 or wider, within the bound.
A program may use at most 128 MiB of HBM per device.

```python
import math
import jax
import jax.numpy as jnp
from jax import lax

BLOCK = 128
DH = 128
HEADS = 16
RAND = 3
GLOB = 2
WMAX = 1
HEAD_DEV = 8
QB = 4
NB = 256
TOKENS = 32768
CAP = 2


def base_pair(key):
    shape = (TOKENS, HEADS * DH)
    key_part = jax.random.fold_in(key, 101)
    query_part = jax.random.fold_in(key, 202)
    key_base = jax.random.truncated_normal(key_part, -6.0, 6.0, shape, jnp.float32)
    query_base = jax.random.truncated_normal(query_part, -6.0, 6.0, shape, jnp.float32)
    return (key_base, query_base)


def draw_keys(key, part):
    key_base, query_base = base_pair(key)
    return key_base.astype(jnp.bfloat16)


def draw_queries(key, part):
    key_base, query_base = base_pair(key)
    return query_base.astype(jnp.bfloat16)


def draw_rand_ids(key, part):
    seq_groups = NB // QB
    head_groups = HEADS // HEAD_DEV
    per_group = HEAD_DEV * QB * RAND
    slot_total = seq_groups * CAP

    def one_group(group_key):
        key_order, key_first, key_shuffle, key_local = jax.random.split(group_key, 4)
        order = jax.random.permutation(key_order, slot_total).astype(jnp.int32)
        first = jax.random.randint(key_first, (), 0, seq_groups)
        positions = jnp.arange(slot_total, dtype=jnp.int32)
        score = jnp.where(positions // CAP == first, -1, order)
        chosen = jnp.argsort(score, stable=True)[:per_group].astype(jnp.int32)
        chosen = jax.random.permutation(key_shuffle, chosen)
        local_ids = jax.random.randint(key_local, (per_group,), 0, QB)
        return chosen // CAP * QB + local_ids
    group_keys = jax.random.split(key, seq_groups * head_groups)
    table = jax.vmap(one_group)(group_keys)
    table = table.reshape(seq_groups, head_groups, HEAD_DEV, QB, RAND).transpose(1, 2, 0, 3, 4)
    return table.reshape(HEADS, NB, RAND).astype(jnp.int32)


def draw_glob_ids(key, part):
    others = jax.random.permutation(jax.random.fold_in(key, 7), NB - 1)[:GLOB - 1].astype(jnp.int32)
    listed = jnp.concatenate([others, jnp.full((1,), NB - 1, jnp.int32)])
    return jax.random.permutation(jax.random.fold_in(key, 11), listed).astype(jnp.int32)


def block_scale(rng, extent, cuts, smallest, largest):
    loudness = 1.0
    for position, parts in cuts:
        steps = jax.random.uniform(jax.random.fold_in(jax.random.fold_in(rng, 6), position), (parts,), jnp.float32, smallest / len(cuts), largest / len(cuts))
        loudness = loudness * jnp.repeat(jnp.exp(steps), extent[position] // parts).reshape((-1,) + (1,) * (len(extent) - 1 - position))
    return loudness


def noise(rng, dims, deviation, reach, cuts=(), kind=jnp.bfloat16):
    factor_of = block_scale(rng, dims, cuts, -0.22, 0.18) if cuts else 1.0
    drawn = jax.random.normal(rng, dims, jnp.float32) * deviation * factor_of
    return jnp.minimum(jnp.maximum(drawn, -reach), reach).astype(kind)


def setup_inputs(seed: int = 0) -> dict:
    key_list = jax.random.split(jax.random.key(seed), 7)
    return {
        "queries": draw_queries(jax.random.fold_in(key_list[6], 71), 0),
        "keys": draw_keys(jax.random.fold_in(key_list[6], 71), 0),
        "values": noise(key_list[2], (TOKENS, HEADS * DH), 1.0, 6.0, ((0, 64), (1, 2))),
        "out_grad": noise(key_list[3], (TOKENS, HEADS * DH), 1.0, 6.0, ((0, 64), (1, 2))),
        "rand_ids": draw_rand_ids(jax.random.fold_in(key_list[6], 71), 0),
        "glob_ids": draw_glob_ids(jax.random.fold_in(key_list[6], 71), 0),
    }


masked_value = -1e+30

def head_terms(query_per_head, key_head, value_head, gradient_per_head, ids_head, glob_ids):
    block_count = query_per_head.shape[0]
    score_scale = 1.0 / math.sqrt(DH)
    window_span = 2 * WMAX + 1
    padding = ((WMAX, WMAX), (0, 0), (0, 0))

    def listed_blocks(whole):
        padded = jnp.pad(whole, padding)
        windowed = jnp.stack([padded[offset:offset + block_count] for offset in range(window_span)], axis=1)
        chosen = whole[ids_head]
        spread = jnp.broadcast_to(whole[glob_ids][None], (block_count, GLOB, BLOCK, DH))
        return jnp.concatenate([windowed, chosen, spread], axis=1).astype(jnp.float32)
    gathered_key_blocks = listed_blocks(key_head)
    gathered_value_blocks = listed_blocks(value_head)
    offsets = jnp.arange(window_span, dtype=jnp.int32) - WMAX
    positions = jnp.arange(block_count, dtype=jnp.int32)[:, None] + offsets[None, :]
    live_window = (positions >= 0) & (positions < block_count)
    live_mask = jnp.concatenate([live_window, jnp.ones((block_count, RAND + GLOB), bool)], axis=1)
    query_wide_float = query_per_head.astype(jnp.float32)
    gradient_wide_float = gradient_per_head.astype(jnp.float32)
    unscaled_scores = jnp.einsum('zjs,zcls->zjcl', query_wide_float, gathered_key_blocks) * score_scale
    unscaled_scores = jnp.where(live_mask[:, None, :, None], unscaled_scores, masked_value)
    peak = lax.optimization_barrier(jnp.max(unscaled_scores, axis=(2, 3), keepdims=True))
    exponent = jnp.exp(unscaled_scores - peak)
    weights = exponent / lax.optimization_barrier(jnp.sum(exponent, axis=(2, 3), keepdims=True))
    weights_narrow_float = lax.optimization_barrier(weights.astype(jnp.bfloat16)).astype(jnp.float32)
    output_per_head = jnp.einsum('qhgf,qgfm->qhm', weights_narrow_float, gathered_value_blocks).astype(jnp.bfloat16)
    out_float = lax.optimization_barrier(output_per_head).astype(jnp.float32)
    row_delta = lax.optimization_barrier(jnp.sum(gradient_wide_float * out_float, axis=-1))
    probability_gradient = jnp.einsum('zjs,zcls->zjcl', gradient_wide_float, gathered_value_blocks)
    score_grad = weights * (probability_gradient - row_delta[:, :, None, None])
    score_narrow_float = lax.optimization_barrier(score_grad.astype(jnp.bfloat16)).astype(jnp.float32)
    query_gradient = (jnp.einsum('qhgf,qgfm->qhm', score_narrow_float, gathered_key_blocks) * score_scale).astype(jnp.bfloat16)
    key_gradient_parts = jnp.einsum('yelt,yev->yltv', score_narrow_float, query_wide_float) * score_scale
    value_gradient_parts = jnp.einsum('yelt,yev->yltv', weights_narrow_float, gradient_wide_float)

    def collect(terms):
        band_total = jnp.zeros((block_count + 2 * WMAX, BLOCK, DH), jnp.float32)
        for offset in range(window_span):
            band_total = band_total + jnp.pad(terms[:, offset], ((offset, window_span - 1 - offset), (0, 0), (0, 0)))
        total = band_total[WMAX:WMAX + block_count]
        rand_low = lax.optimization_barrier(terms[:, window_span:window_span + RAND].astype(jnp.bfloat16)).astype(jnp.float32)
        total = total.at[ids_head].add(rand_low)
        total = total.at[glob_ids].add(lax.optimization_barrier(jnp.sum(terms[:, window_span + RAND:], axis=0)))
        return total.astype(jnp.bfloat16)
    return (output_per_head, query_gradient, collect(key_gradient_parts), collect(value_gradient_parts))

def reference(queries, keys, values, out_grad, rand_ids, glob_ids):

    def split(array):
        return array.reshape(NB, BLOCK, HEADS, DH).transpose(2, 0, 1, 3)

    def one_head(operands):
        return head_terms(operands[0], operands[1], operands[2], operands[3], operands[4], glob_ids)
    results = lax.map(one_head, (split(queries), split(keys), split(values), split(out_grad), rand_ids))

    def join(array):
        return array.transpose(1, 2, 0, 3).reshape(NB * BLOCK, HEADS * DH)
    return (join(results[0]), join(results[1]), join(results[2]), join(results[3]))
```

```python
import functools
import math

import jax
import jax.numpy as jnp
from jax import lax
from jax.experimental import pallas as pl
from jax.experimental.pallas import tpu as pltpu
from jax.sharding import PartitionSpec as P

BLOCK = 128
DH = 128
RAND = 3
HEADS_HERE = 8
QB = 4
SHARDS = 64
ENTRIES = HEADS_HERE * QB * RAND
NONE = 1 << 20
LAST = SHARDS - 1
GROWS = HEADS_HERE * 2 * BLOCK
PIECE = GROWS // SHARDS
QUART = GROWS // 4
SCALE = 1.0 / math.sqrt(DH)
MASKED = -1e30
MESH = pl.DeviceIdType.MESH
ANY = pl.ANY
BF = jnp.bfloat16
F32 = jnp.float32


def orbits():
    def key(d):
        return (d // 16, (d // 4) % 4, d % 4)

    def hops(d):
        return sum(min(v, 4 - v) for v in key(d))

    seen, rounds = set(), []
    for d in sorted(range(1, SHARDS), key=lambda d: (hops(d), d)):
        if d in seen:
            continue
        orbit = []
        for turn in range(3):
            k = key(d)[turn:] + key(d)[:turn]
            for sign in (1, -1):
                a, b, c = ((sign * v) % 4 for v in k)
                if a * 16 + b * 4 + c not in orbit:
                    orbit.append(a * 16 + b * 4 + c)
        seen.update(orbit)
        rounds.append(orbit)
    return rounds


ROUNDS = orbits()


def moved(me, d, sign=1):
    y, z, x = lax.div(me, 16), lax.rem(lax.div(me, 4), 4), lax.rem(me, 4)
    dy, dz, dx = lax.div(d, 16), lax.rem(lax.div(d, 4), 4), lax.rem(d, 4)
    if sign < 0:
        dy, dz, dx = 4 - dy, 4 - dz, 4 - dx
    return lax.rem(y + dy, 4) * 16 + lax.rem(z + dz, 4) * 4 + lax.rem(x + dx, 4)


def shifted(me, d, sign=1):
    dy, dz, dx = d // 16, (d // 4) % 4, d % 4
    if sign < 0:
        dy, dz, dx = 4 - dy, 4 - dz, 4 - dx
    y, z, x = lax.div(me, 16), lax.rem(lax.div(me, 4), 4), lax.rem(me, 4)
    return lax.rem(y + dy, 4) * 16 + lax.rem(z + dz, 4) * 4 + lax.rem(x + dx, 4)


def remote(src, dst, send, recv, target):
    return pltpu.make_async_remote_copy(
        src_ref=src,
        dst_ref=dst,
        send_sem=send,
        recv_sem=recv,
        device_id={"seq": target},
        device_id_type=MESH,
    )


def enter(me):
    barrier = pltpu.get_barrier_semaphore()

    def greet(d, carry):
        pl.semaphore_signal(
            barrier, inc=1, device_id={"seq": moved(me, d)}, device_id_type=MESH
        )
        return carry

    lax.fori_loop(1, SHARDS, greet, 0)
    pl.semaphore_wait(barrier, SHARDS - 1)


def prep_kernel(cmin, cmax, misc, k_ref, v_ref, payload, cand_o, cand_l, sem, gsem):
    me = lax.axis_index("seq")

    def put(d, carry):
        t = moved(me, d)
        low = cmin[t]
        high = cmax[t]
        for c, code in ((0, jnp.where(low < NONE, low, 0)), (1, jnp.maximum(high, 0))):
            head = lax.div(code, 4 * QB * RAND)
            blk = lax.rem(code, 4)
            rows = pl.ds(pl.multiple_of(blk * BLOCK, BLOCK), BLOCK)
            cols = pl.ds(pl.multiple_of(head * DH, DH), DH)
            pltpu.make_async_copy(k_ref.at[rows, cols], payload.at[d, c, 0], sem).start()
            pltpu.make_async_copy(v_ref.at[rows, cols], payload.at[d, c, 1], sem).start()
        return carry

    rows_o = pl.ds(pl.multiple_of(misc[0] * BLOCK, BLOCK), BLOCK)
    rows_l = pl.ds((QB - 1) * BLOCK, BLOCK)
    for h in range(HEADS_HERE):
        cols = pl.ds(h * DH, DH)
        for kv, ref in ((0, k_ref), (1, v_ref)):
            dst = pl.ds((2 * h + kv) * BLOCK, BLOCK)
            pltpu.make_async_copy(ref.at[rows_o, cols], cand_o.at[dst], gsem.at[0]).start()
            pltpu.make_async_copy(ref.at[rows_l, cols], cand_l.at[dst], gsem.at[1]).start()
    lax.fori_loop(0, SHARDS, put, 0)
    pltpu.make_async_copy(cand_o, cand_o, gsem.at[0]).wait()
    pltpu.make_async_copy(cand_l, cand_l, gsem.at[1]).wait()
    pltpu.make_async_copy(payload, payload, sem).wait()


def send_round(me, sign, src, dst, ss, rs, offsets):
    def piece(i, carry):
        c, kv = lax.div(i, 2), lax.rem(i, 2)
        for d in offsets:
            remote(
                src.at[d, c, kv], dst.at[d, c, kv], ss.at[d], rs.at[d], shifted(me, d, sign)
            ).start()
        return carry

    lax.fori_loop(0, 4, piece, 0)


def sent_round(me, src, dst, ss, rs, offsets):
    for d in offsets:
        remote(src.at[d], dst.at[d], ss.at[d], rs.at[d], me).wait_send()


def arrived_round(me, src, dst, ss, rs, offsets):
    for d in offsets:
        remote(src.at[d], dst.at[d], ss.at[d], rs.at[d], me).wait_recv()


def plane_target(me, dp):
    return shifted(me, dp)


def fetch_kernel(
    sel, payload, k_ref, v_ref, cand_o, cand_l, recv, halo, gfull,
    ay, gq, ap, ss, rs, hs, hr, ys, yr, ps, pr, ls, lr, bs, br, cs, cr, own_sem,
):
    me = lax.axis_index("seq")
    y = lax.div(me, 16)
    plane = lax.rem(me, 16)
    enter(me)
    after = lax.rem(me + 1, SHARDS)
    before = lax.rem(me + SHARDS - 1, SHARDS)
    own = pltpu.make_async_copy(payload.at[0], recv.at[0], own_sem)
    own.start()

    up = []
    for dy in range(1, 4):
        ty = lax.rem(y + dy, 4)
        copy = remote(
            cand_o.at[pl.ds(pl.multiple_of(ty * QUART, QUART), QUART)],
            ay.at[dy], ys.at[dy], yr.at[dy], ty * 16 + plane,
        )
        copy.start()
        up.append(copy)

    @pl.when(me == LAST)
    def _():
        def scatter(t, carry):
            rows = pl.ds(pl.multiple_of(t * PIECE, PIECE), PIECE)
            remote(cand_l.at[rows], gfull.at[1, rows], ls.at[t], lr, t).start()
            return carry

        lax.fori_loop(0, LAST, scatter, 0)
        gfull[1, pl.ds(LAST * PIECE, PIECE), :] = cand_l[pl.ds(LAST * PIECE, PIECE), :]

    halos = []
    for kv, ref in ((0, k_ref), (1, v_ref)):
        for side, rows, target in (
            (0, pl.ds((QB - 1) * BLOCK, BLOCK), after),
            (1, pl.ds(0, BLOCK), before),
        ):
            copy = remote(
                ref.at[rows], halo.at[side, kv], hs.at[2 * side + kv], hr.at[2 * side + kv], target
            )
            copy.start()
            halos.append(copy)

    ay[0] = cand_o[pl.ds(pl.multiple_of(y * QUART, QUART), QUART), :]
    mine = pl.ds(pl.multiple_of(me * PIECE, PIECE), PIECE)
    quarter = pl.ds(pl.multiple_of(y * QUART, QUART), QUART)
    across, spread, raised = [], [], []
    for number, offsets in enumerate(ROUNDS):
        if number >= 2:
            sent_round(me, payload, recv, ss, rs, ROUNDS[number - 2])
        send_round(me, 1, payload, recv, ss, rs, offsets)
        if number == 2:
            for copy in up:
                copy.wait_recv()
            gq[...] = ay[sel[0]]
        if number == 3:
            for dp in range(1, 16):
                target = plane_target(me, dp)
                rows = pl.ds(pl.multiple_of(lax.rem(target, 16) * PIECE, PIECE), PIECE)
                copy = remote(gq.at[rows], ap.at[dp], ps.at[dp], pr.at[dp], target)
                copy.start()
                across.append(copy)
            ap[0] = gq[pl.ds(pl.multiple_of(plane * PIECE, PIECE), PIECE), :]
        if number == 5:
            for copy in across:
                copy.wait_recv()
            gfull[0, mine, :] = ap[sel[1]]

            @pl.when(me != LAST)
            def _():
                remote(cand_l.at[mine], gfull.at[1, mine], ls.at[0], lr, me).wait_recv()

        if number == 6:
            for dp in range(1, 16):
                copy = remote(
                    gfull.at[:, mine], gfull.at[:, mine], bs.at[dp], br.at[dp], plane_target(me, dp)
                )
                copy.start()
                spread.append(copy)
        if number == 8:
            for copy in spread:
                copy.wait_recv()
            for dy in range(1, 4):
                copy = remote(
                    gfull.at[:, quarter], gfull.at[:, quarter], cs.at[dy], cr.at[dy],
                    lax.rem(y + dy, 4) * 16 + plane,
                )
                copy.start()
                raised.append(copy)
    for offsets in ROUNDS[-2:]:
        sent_round(me, payload, recv, ss, rs, offsets)
    for offsets in ROUNDS:
        arrived_round(me, payload, recv, ss, rs, offsets)
    for copy in up + across + spread:
        copy.wait_send()
    for copy in raised + halos:
        copy.wait()

    @pl.when(me == LAST)
    def _():
        def done(t, carry):
            rows = pl.ds(pl.multiple_of(t * PIECE, PIECE), PIECE)
            remote(cand_l.at[rows], gfull.at[1, rows], ls.at[t], lr, t).wait_send()
            return carry

        lax.fori_loop(0, LAST, done, 0)

    own.wait()


def nt(a, b):
    return lax.dot_general(a, b, (((1,), (1,)), ((), ())), preferred_element_type=F32)


def nn(a, b):
    return lax.dot_general(a, b, (((1,), (0,)), ((), ())), preferred_element_type=F32)


def tn(a, b):
    return lax.dot_general(a, b, (((0,), (0,)), ((), ())), preferred_element_type=F32)


def attend_kernel(
    pick, q_ref, k_ref, v_ref, g_ref, halo_ref, glob_ref, recv,
    out_ref, dq_ref, center_ref, rim_ref, gpart_ref, outgoing,
    rk, rv, tk, tv, bandk, bandv, gk, gv, acck, accv, dsg, pgs, in_sem, out_sem,
):
    me = lax.axis_index("seq")
    h = pl.program_id(0)
    slot = lax.rem(h, 2)
    per_head = QB * RAND

    def load(head, buf):
        for e in range(per_head):
            s = pick[head * per_head + e]
            d, c = lax.div(s, 2), lax.rem(s, 2)
            rows = pl.ds(e * BLOCK, BLOCK)
            pltpu.make_async_copy(recv.at[d, c, 0], rk.at[buf, rows], in_sem.at[buf]).start()
            pltpu.make_async_copy(recv.at[d, c, 1], rv.at[buf, rows], in_sem.at[buf]).start()

    def drain(buf):
        pltpu.make_async_copy(tk.at[buf], tk.at[buf], out_sem.at[buf]).wait()
        pltpu.make_async_copy(tv.at[buf], tv.at[buf], out_sem.at[buf]).wait()

    @pl.when(h == 0)
    def _():
        load(0, 0)

    @pl.when(h + 1 < HEADS_HERE)
    def _():
        load(h + 1, 1 - slot)

    rows_here = QB * BLOCK
    for band, kv, ref in ((bandk, 0, k_ref), (bandv, 1, v_ref)):
        band[0:BLOCK] = halo_ref[0, kv]
        band[BLOCK : BLOCK + rows_here] = ref[...]
        band[BLOCK + rows_here :] = halo_ref[1, kv]
    for g in range(2):
        gk[g * BLOCK : (g + 1) * BLOCK] = glob_ref[g, 0, 0]
        gv[g * BLOCK : (g + 1) * BLOCK] = glob_ref[g, 0, 1]
    acck[...] = jnp.zeros_like(acck)
    accv[...] = jnp.zeros_like(accv)
    pltpu.make_async_copy(rk.at[slot], rk.at[slot], in_sem.at[slot]).wait()
    pltpu.make_async_copy(rv.at[slot], rv.at[slot], in_sem.at[slot]).wait()

    @pl.when(h >= 2)
    def _():
        drain(slot)

    span = 3 * BLOCK
    col = lax.broadcasted_iota(jnp.int32, (BLOCK, span), 1)
    for i in range(QB):
        mine = slice(i * BLOCK, (i + 1) * BLOCK)
        q = q_ref[mine, :]
        g = g_ref[mine, :]
        wk, wv = bandk[i * BLOCK : i * BLOCK + span], bandv[i * BLOCK : i * BLOCK + span]
        ek, ev = rk[slot, i * span : (i + 1) * span], rv[slot, i * span : (i + 1) * span]
        sw = nt(q, wk) * SCALE
        if i == 0:
            sw = jnp.where((col < BLOCK) & (me == 0), MASKED, sw)
        if i == QB - 1:
            sw = jnp.where((col >= 2 * BLOCK) & (me == LAST), MASKED, sw)
        sr = nt(q, ek) * SCALE
        sg = nt(q, gk[...]) * SCALE
        peak = jnp.maximum(
            jnp.maximum(jnp.max(sw, axis=1, keepdims=True), jnp.max(sr, axis=1, keepdims=True)),
            jnp.max(sg, axis=1, keepdims=True),
        )
        sw, sr, sg = jnp.exp(sw - peak), jnp.exp(sr - peak), jnp.exp(sg - peak)
        total = (
            jnp.sum(sw, axis=1, keepdims=True)
            + jnp.sum(sr, axis=1, keepdims=True)
            + jnp.sum(sg, axis=1, keepdims=True)
        )
        inverse = 1.0 / total
        sw, sr, sg = sw * inverse, sr * inverse, sg * inverse
        pw, pr, pg = sw.astype(BF), sr.astype(BF), sg.astype(BF)
        out = (nn(pw, wv) + nn(pr, ev) + nn(pg, gv[...])).astype(BF)
        out_ref[mine, :] = out
        delta = jnp.sum(g.astype(F32) * out.astype(F32), axis=1, keepdims=True)
        dw = (sw * (nt(g, wv) - delta)).astype(BF)
        dr = (sr * (nt(g, ev) - delta)).astype(BF)
        dg = (sg * (nt(g, gv[...]) - delta)).astype(BF)
        dq_ref[mine, :] = ((nn(dw, wk) + nn(dr, ek) + nn(dg, gk[...])) * SCALE).astype(BF)
        acck[i * BLOCK : i * BLOCK + span] += tn(dw, q)
        accv[i * BLOCK : i * BLOCK + span] += tn(pw, g)
        tk[slot, i * span : (i + 1) * span] = (tn(dr, q) * SCALE).astype(BF)
        tv[slot, i * span : (i + 1) * span] = tn(pr, g).astype(BF)
        dsg[mine, :] = dg
        pgs[mine, :] = pg
    gdk = tn(dsg[...], q_ref[...]) * SCALE
    gdv = tn(pgs[...], g_ref[...])
    for g in range(2):
        gpart_ref[g, 0, 0] = gdk[g * BLOCK : (g + 1) * BLOCK].astype(BF)
        gpart_ref[g, 0, 1] = gdv[g * BLOCK : (g + 1) * BLOCK].astype(BF)
    center_ref[0] = acck[BLOCK : BLOCK + rows_here] * SCALE
    center_ref[1] = accv[BLOCK : BLOCK + rows_here]
    rim_ref[0, 0] = (acck[0:BLOCK] * SCALE).astype(BF)
    rim_ref[0, 1] = accv[0:BLOCK].astype(BF)
    rim_ref[1, 0] = (acck[BLOCK + rows_here :] * SCALE).astype(BF)
    rim_ref[1, 1] = accv[BLOCK + rows_here :].astype(BF)
    for e in range(per_head):
        s = pick[h * per_head + e]
        d, c = lax.div(s, 2), lax.rem(s, 2)
        rows = pl.ds(e * BLOCK, BLOCK)
        pltpu.make_async_copy(tk.at[slot, rows], outgoing.at[d, c, 0], out_sem.at[slot]).start()
        pltpu.make_async_copy(tv.at[slot, rows], outgoing.at[d, c, 1], out_sem.at[slot]).start()

    @pl.when(h == HEADS_HERE - 1)
    def _():
        drain(1 - slot)
        drain(slot)


def return_kernel(
    outgoing, rim, gpart, returned, rim_back, gtot, glast,
    ry, g1, rp, g2, ss, rs, hs, hr, ys, yr, ps, pr, ls, lr, bs, br, cs, cr, own_sem,
):
    me = lax.axis_index("seq")
    y = lax.div(me, 16)
    plane = lax.rem(me, 16)
    enter(me)
    after = lax.rem(me + 1, SHARDS)
    before = lax.rem(me + SHARDS - 1, SHARDS)
    own = pltpu.make_async_copy(outgoing.at[0], returned.at[0], own_sem)
    own.start()
    up = []
    for dy in range(1, 4):
        ty = lax.rem(y + dy, 4)
        copy = remote(
            gpart.at[:, pl.ds(pl.multiple_of(ty * QUART, QUART), QUART)],
            ry.at[dy - 1], ys.at[dy], yr.at[dy], ty * 16 + plane,
        )
        copy.start()
        up.append(copy)
    halos = []
    for kv in range(2):
        for side, target in ((0, before), (1, after)):
            copy = remote(
                rim.at[side, kv], rim_back.at[1 - side, kv],
                hs.at[2 * side + kv], hr.at[2 * side + kv], target,
            )
            copy.start()
            halos.append(copy)
    mine = pl.ds(pl.multiple_of(me * PIECE, PIECE), PIECE)
    quarter = pl.ds(pl.multiple_of(y * QUART, QUART), QUART)
    part = pl.ds(pl.multiple_of(plane * PIECE, PIECE), PIECE)
    across, spread, raised = [], [], []
    for number, offsets in enumerate(ROUNDS):
        if number >= 2:
            sent_round(me, outgoing, returned, ss, rs, ROUNDS[number - 2])
        send_round(me, -1, outgoing, returned, ss, rs, offsets)
        if number == 3:
            for copy in up:
                copy.wait_recv()
            for g in range(2):
                g1[g] = (
                    gpart[g, quarter, :].astype(F32)
                    + ry[0, g].astype(F32)
                    + ry[1, g].astype(F32)
                    + ry[2, g].astype(F32)
                ).astype(BF)
        if number == 4:
            for dp in range(1, 16):
                target = plane_target(me, dp)
                rows = pl.ds(pl.multiple_of(lax.rem(target, 16) * PIECE, PIECE), PIECE)
                copy = remote(g1.at[:, rows], rp.at[dp], ps.at[dp], pr.at[dp], target)
                copy.start()
                across.append(copy)
        if number == 6:
            for copy in across:
                copy.wait_recv()
            total = g1[:, part, :].astype(F32)
            for dp in range(1, 16):
                total = total + rp[dp].astype(F32)
            g2[...] = total.astype(BF)
            gtot[mine, :] = total[0].astype(BF)
        if number == 7:

            @pl.when(me != LAST)
            def _():
                remote(g2.at[1], glast.at[mine], ls, lr.at[me], LAST).start()

            @pl.when(me == LAST)
            def _():
                glast[mine, :] = g2[1]

            for dp in range(1, 16):
                copy = remote(
                    gtot.at[mine], gtot.at[mine], bs.at[dp], br.at[dp], plane_target(me, dp)
                )
                copy.start()
                spread.append(copy)
        if number == 9:
            for copy in spread:
                copy.wait_recv()
            for dy in range(1, 4):
                copy = remote(
                    gtot.at[quarter], gtot.at[quarter], cs.at[dy], cr.at[dy],
                    lax.rem(y + dy, 4) * 16 + plane,
                )
                copy.start()
                raised.append(copy)
    for offsets in ROUNDS[-2:]:
        sent_round(me, outgoing, returned, ss, rs, offsets)
    for offsets in ROUNDS:
        arrived_round(me, outgoing, returned, ss, rs, offsets)
    for copy in up + across + spread:
        copy.wait_send()
    for copy in raised + halos:
        copy.wait()

    @pl.when(me != LAST)
    def _():
        remote(g2.at[1], glast.at[mine], ls, lr.at[me], LAST).wait_send()

    @pl.when(me == LAST)
    def _():
        def done(t, carry):
            rows = pl.ds(pl.multiple_of(t * PIECE, PIECE), PIECE)
            remote(g2.at[1], glast.at[rows], ls, lr.at[t], t).wait_recv()
            return carry

        lax.fori_loop(0, LAST, done, 0)

    own.wait()


CHUNK = 4


def collect_kernel(
    cmin, cmax, misc, center, rim, gtot, glast, returned, dk_ref, dv_ref, buf, acc, sem, csem
):
    me = lax.axis_index("seq")
    steps = SHARDS // CHUNK

    def fetch(step, slot):
        return pltpu.make_async_copy(
            returned.at[pl.ds(step * CHUNK, CHUNK)], buf.at[slot], sem.at[slot]
        )

    whole = pltpu.make_async_copy(center, acc, csem)
    whole.start()
    fetch(0, 0).start()
    whole.wait()
    for kv in range(2):
        acc[kv, 0:BLOCK, :] += rim[0, kv].astype(F32)
        acc[kv, (QB - 1) * BLOCK :, :] += rim[1, kv].astype(F32)

    def add_glob(blk, ref):
        rows = pl.ds(pl.multiple_of(blk * BLOCK, BLOCK), BLOCK)
        for h in range(HEADS_HERE):
            for kv in range(2):
                src = ref[pl.ds((2 * h + kv) * BLOCK, BLOCK), :]
                acc[kv, rows, pl.ds(h * DH, DH)] += src.astype(F32)

    @pl.when(me == LAST)
    def _():
        add_glob(QB - 1, glast)

    @pl.when(me == misc[1])
    def _():
        add_glob(misc[0], gtot)

    def add(code, slot, place, c):
        head = lax.div(code, 4 * QB * RAND)
        blk = lax.rem(code, 4)
        rows = pl.ds(pl.multiple_of(blk * BLOCK, BLOCK), BLOCK)
        cols = pl.ds(pl.multiple_of(head * DH, DH), DH)
        for kv in range(2):
            acc[kv, rows, cols] += buf[slot, place, c, kv].astype(F32)

    def step_body(step, carry):
        slot = lax.rem(step, 2)

        @pl.when(step + 1 < steps)
        def _():
            fetch(step + 1, 1 - slot).start()

        fetch(step, slot).wait()
        for place in range(CHUNK):
            t = moved(me, step * CHUNK + place)
            low, high = cmin[t], cmax[t]

            @pl.when(low < NONE)
            def _():
                add(low, slot, place, 0)

            @pl.when(high > low)
            def _():
                add(high, slot, place, 1)

        return carry

    lax.fori_loop(0, steps, step_body, 0)
    dk_ref[...] = acc[0].astype(BF)
    dv_ref[...] = acc[1].astype(BF)


def smem():
    return pl.BlockSpec(memory_space=pltpu.SMEM)


def vmem():
    return pl.BlockSpec(memory_space=pltpu.VMEM)


def hbm():
    return pl.BlockSpec(memory_space=ANY)


def dma(*shape):
    return pltpu.SemaphoreType.DMA(shape)


def body(queries, keys, values, out_grad, rand_ids, glob_ids):
    place = lax.axis_index("seq")
    group = lax.axis_index("head")
    shape = jax.ShapeDtypeStruct
    ids = lax.dynamic_slice_in_dim(rand_ids, group * HEADS_HERE, HEADS_HERE, 0)
    ids = ids.reshape(HEADS_HERE, SHARDS, QB * RAND)
    number = (
        jnp.arange(HEADS_HERE, dtype=jnp.int32)[:, None, None] * (QB * RAND)
        + jnp.arange(QB * RAND, dtype=jnp.int32)[None, None, :]
    )
    code = number * 4 + lax.rem(ids, 4)
    hit = lax.div(ids, 4) == place
    cmin = jnp.min(jnp.where(hit, code, NONE), axis=(0, 2))
    cmax = jnp.max(jnp.where(hit, code, -1), axis=(0, 2))
    own = lax.dynamic_index_in_dim(ids, place, 1, False).reshape(ENTRIES)
    src = lax.div(own, 4)
    order = jnp.arange(ENTRIES, dtype=jnp.int32)
    again = jnp.any((src[:, None] == src[None, :]) & (order[None, :] < order[:, None]), axis=1)

    def part(value, step):
        return lax.rem(lax.div(value, step), 4)

    def away(a, b):
        return sum(lax.rem(part(a, s) - part(b, s) + 4, 4) * s for s in (16, 4, 1))

    pick = away(place, src) * 2 + again.astype(jnp.int32)
    other = glob_ids[0] + glob_ids[1] - (SHARDS * QB - 1)
    root = lax.div(other, QB)
    misc = jnp.stack([lax.rem(other, QB), root])
    sel = jnp.stack([lax.div(away(place, root), 16), lax.rem(away(place, root), 16)])
    slots = shape((SHARDS, 2, 2, BLOCK, DH), BF)
    width = HEADS_HERE * DH
    rows_here = QB * BLOCK

    payload, cand_o, cand_l = pl.pallas_call(
        prep_kernel,
        out_shape=(slots, shape((GROWS, DH), BF), shape((GROWS, DH), BF)),
        in_specs=[smem(), smem(), smem(), vmem(), vmem()],
        out_specs=(hbm(), hbm(), hbm()),
        scratch_shapes=[pltpu.SemaphoreType.DMA, dma(2)],
        name="prep",
    )(cmin, cmax, misc, keys, values)

    recv, halo, gfull = pl.pallas_call(
        fetch_kernel,
        out_shape=(slots, shape((2, 2, BLOCK, width), BF), shape((2, GROWS, DH), BF)),
        in_specs=[smem(), hbm(), hbm(), hbm(), vmem(), vmem()],
        out_specs=(hbm(), hbm(), vmem()),
        scratch_shapes=[
            pltpu.VMEM((4, QUART, DH), BF),
            pltpu.VMEM((QUART, DH), BF),
            pltpu.VMEM((16, PIECE, DH), BF),
            dma(SHARDS), dma(SHARDS), dma(4), dma(4), dma(4), dma(4), dma(16), dma(16),
            dma(SHARDS), pltpu.SemaphoreType.DMA, dma(16), dma(16), dma(4), dma(4),
            pltpu.SemaphoreType.DMA,
        ],
        compiler_params=pltpu.CompilerParams(collective_id=0, has_side_effects=True),
        name="fetch",
    )(sel, payload, keys, values, cand_o, cand_l)

    span = 3 * BLOCK
    head_block = pl.BlockSpec((rows_here, DH), lambda h, *_: (0, h))
    side_block = pl.BlockSpec((2, 2, BLOCK, DH), lambda h, *_: (0, 0, 0, h))
    glob_block = pl.BlockSpec((2, 1, 2, BLOCK, DH), lambda h, *_: (0, h, 0, 0, 0))
    full = QB * span
    out, dq, center, rim, gpart, outgoing = pl.pallas_call(
        attend_kernel,
        out_shape=(
            shape((rows_here, width), BF),
            shape((rows_here, width), BF),
            shape((2, rows_here, width), F32),
            shape((2, 2, BLOCK, width), BF),
            shape((2, HEADS_HERE, 2, BLOCK, DH), BF),
            slots,
        ),
        grid_spec=pltpu.PrefetchScalarGridSpec(
            num_scalar_prefetch=1,
            grid=(HEADS_HERE,),
            in_specs=[head_block] * 4 + [side_block, glob_block, hbm()],
            out_specs=[
                head_block,
                head_block,
                pl.BlockSpec((2, rows_here, DH), lambda h, *_: (0, 0, h)),
                side_block,
                glob_block,
                hbm(),
            ],
            scratch_shapes=[pltpu.VMEM((2, full, DH), BF)] * 4
            + [pltpu.VMEM((rows_here + 2 * BLOCK, DH), BF)] * 2
            + [pltpu.VMEM((2 * BLOCK, DH), BF)] * 2
            + [pltpu.VMEM((rows_here + 2 * BLOCK, DH), F32)] * 2
            + [pltpu.VMEM((rows_here, 2 * BLOCK), BF)] * 2
            + [dma(2), dma(2)],
        ),
        name="attend",
    )(
        pick, queries, keys, values, out_grad, halo,
        gfull.reshape(2, HEADS_HERE, 2, BLOCK, DH), recv,
    )

    returned, rim_back, gtot, glast = pl.pallas_call(
        return_kernel,
        out_shape=(
            slots,
            shape((2, 2, BLOCK, width), BF),
            shape((GROWS, DH), BF),
            shape((GROWS, DH), BF),
        ),
        in_specs=[hbm(), hbm(), vmem()],
        out_specs=(hbm(), hbm(), vmem(), vmem()),
        scratch_shapes=[
            pltpu.VMEM((3, 2, QUART, DH), BF),
            pltpu.VMEM((2, QUART, DH), BF),
            pltpu.VMEM((16, 2, PIECE, DH), BF),
            pltpu.VMEM((2, PIECE, DH), BF),
            dma(SHARDS), dma(SHARDS), dma(4), dma(4), dma(4), dma(4), dma(16), dma(16),
            pltpu.SemaphoreType.DMA, dma(SHARDS), dma(16), dma(16), dma(4), dma(4),
            pltpu.SemaphoreType.DMA,
        ],
        compiler_params=pltpu.CompilerParams(collective_id=1, has_side_effects=True),
        name="return",
    )(outgoing, rim, gpart.reshape(2, GROWS, DH))

    dk, dv = pl.pallas_call(
        collect_kernel,
        out_shape=(shape((rows_here, width), BF), shape((rows_here, width), BF)),
        in_specs=[smem(), smem(), smem(), hbm(), vmem(), vmem(), vmem(), hbm()],
        out_specs=(vmem(), vmem()),
        scratch_shapes=[
            pltpu.VMEM((2, CHUNK, 2, 2, BLOCK, DH), BF),
            pltpu.VMEM((2, rows_here, width), F32),
            dma(2),
            pltpu.SemaphoreType.DMA,
        ],
        name="collect",
    )(cmin, cmax, misc, center, rim_back, gtot, glast, returned)
    return out, dq, dk, dv


def solution(mesh):
    rows = P("seq", "head")
    return jax.shard_map(
        body,
        mesh=mesh,
        in_specs=(rows, rows, rows, rows, P(), P()),
        out_specs=(rows, rows, rows, rows),
        check_vma=False,
    )
```

```python
import functools
import math

import jax
import jax.numpy as jnp
from jax import lax
from jax.experimental import pallas as pl
from jax.experimental.pallas import tpu as pltpu
from jax.sharding import PartitionSpec as P

BLOCK = 128
DH = 128
RAND = 3
HEADS_HERE = 8
QB = 4
SHARDS = 64
ENTRIES = HEADS_HERE * QB * RAND
NONE = 1 << 20
DEPTH = 6
FETCH_AT = (1, 2, 3, 4, 8)
FAR_AT = (1, 2, 3, 4, 5, 6, 7, 8)
RETURN_AT = (3, 4, 5, 6, 8)
LAST = SHARDS - 1
GROWS = HEADS_HERE * 2 * BLOCK
PIECE = GROWS // SHARDS
QUART = GROWS // 4
SCALE = 1.0 / math.sqrt(DH)
MASKED = -1e30
MESH = pl.DeviceIdType.MESH
ANY = pl.ANY
BF = jnp.bfloat16
F32 = jnp.float32


def orbits():
    def key(d):
        return (d // 16, (d // 4) % 4, d % 4)

    def hops(d):
        return sum(min(v, 4 - v) for v in key(d))

    seen, rounds = set(), []
    for d in sorted(range(1, SHARDS), key=lambda d: (hops(d), d)):
        if d in seen:
            continue
        orbit = []
        for turn in range(3):
            k = key(d)[turn:] + key(d)[:turn]
            for sign in (1, -1):
                a, b, c = ((sign * v) % 4 for v in k)
                if a * 16 + b * 4 + c not in orbit:
                    orbit.append(a * 16 + b * 4 + c)
        seen.update(orbit)
        rounds.append(orbit)
    return rounds


ROUNDS = orbits()


def moved(me, d, sign=1):
    y, z, x = lax.div(me, 16), lax.rem(lax.div(me, 4), 4), lax.rem(me, 4)
    dy, dz, dx = lax.div(d, 16), lax.rem(lax.div(d, 4), 4), lax.rem(d, 4)
    if sign < 0:
        dy, dz, dx = 4 - dy, 4 - dz, 4 - dx
    return lax.rem(y + dy, 4) * 16 + lax.rem(z + dz, 4) * 4 + lax.rem(x + dx, 4)


def shifted(me, d, sign=1):
    dy, dz, dx = d // 16, (d // 4) % 4, d % 4
    if sign < 0:
        dy, dz, dx = 4 - dy, 4 - dz, 4 - dx
    y, z, x = lax.div(me, 16), lax.rem(lax.div(me, 4), 4), lax.rem(me, 4)
    return lax.rem(y + dy, 4) * 16 + lax.rem(z + dz, 4) * 4 + lax.rem(x + dx, 4)


def remote(src, dst, send, recv, target):
    return pltpu.make_async_remote_copy(
        src_ref=src,
        dst_ref=dst,
        send_sem=send,
        recv_sem=recv,
        device_id={"seq": target},
        device_id_type=MESH,
    )


def enter(me):
    barrier = pltpu.get_barrier_semaphore()

    def greet(d, carry):
        pl.semaphore_signal(
            barrier, inc=1, device_id={"seq": moved(me, d)}, device_id_type=MESH
        )
        return carry

    lax.fori_loop(1, SHARDS, greet, 0)
    pl.semaphore_wait(barrier, SHARDS - 1)


def prep_kernel(
    glob, own_ids, ids, k_ref, v_ref, payload, cand_o, cand_l, pick, codes, count, table, sem,
    gsem, tsem,
):
    me = lax.axis_index("seq")
    entry = lax.broadcasted_iota(jnp.int32, (ENTRIES, SHARDS), 0)
    code = entry * 4 + (ids[...] & 3)
    hit = (ids[...] >> 2) == me
    codes[0:1, :] = jnp.min(jnp.where(hit, code, NONE), axis=0, keepdims=True)
    codes[1:2, :] = jnp.max(jnp.where(hit, code, -1), axis=0, keepdims=True)
    to_scalar = pltpu.make_async_copy(codes, table, tsem)
    to_scalar.start()
    other = glob[0] + glob[1] - (SHARDS * QB - 1)
    rows_o = pl.ds(pl.multiple_of(lax.rem(other, QB) * BLOCK, BLOCK), BLOCK)
    rows_l = pl.ds((QB - 1) * BLOCK, BLOCK)
    for h in range(HEADS_HERE):
        cols = pl.ds(h * DH, DH)
        for kv, ref in ((0, k_ref), (1, v_ref)):
            dst = pl.ds((2 * h + kv) * BLOCK, BLOCK)
            pltpu.make_async_copy(ref.at[rows_o, cols], cand_o.at[dst], gsem.at[0]).start()
            pltpu.make_async_copy(ref.at[rows_l, cols], cand_l.at[dst], gsem.at[1]).start()
    to_scalar.wait()

    def put(d, carry):
        t = moved(me, d)
        low = table[0, t]
        high = table[1, t]
        count[t] = 0
        for c, code in ((0, jnp.where(low < NONE, low, 0)), (1, jnp.maximum(high, 0))):
            head = lax.div(code, 4 * QB * RAND)
            blk = lax.rem(code, 4)
            rows = pl.ds(pl.multiple_of(blk * BLOCK, BLOCK), BLOCK)
            cols = pl.ds(pl.multiple_of(head * DH, DH), DH)
            pltpu.make_async_copy(k_ref.at[rows, cols], payload.at[d, c, 0], sem).start()
            pltpu.make_async_copy(v_ref.at[rows, cols], payload.at[d, c, 1], sem).start()
        return carry

    lax.fori_loop(0, SHARDS, put, 0)

    def choose(e, carry):
        src = lax.div(own_ids[e], 4)
        seen = count[src]
        count[src] = seen + 1
        away = 0
        for axis in "yzx":
            gap = lax.rem(place_of(me, axis) + 4 - place_of(src, axis), 4)
            away = away + gap * STEP[axis]
        pick[e] = away * 2 + jnp.minimum(seen, 1)
        return carry

    lax.fori_loop(0, ENTRIES, choose, 0)
    pltpu.make_async_copy(cand_o, cand_o, gsem.at[0]).wait()
    pltpu.make_async_copy(cand_l, cand_l, gsem.at[1]).wait()
    pltpu.make_async_copy(payload, payload, sem).wait()


def send_round(me, sign, src, dst, ss, rs, offsets):
    def piece(i, carry):
        c, kv = lax.div(i, 2), lax.rem(i, 2)
        for d in offsets:
            remote(
                src.at[d, c, kv], dst.at[d, c, kv], ss.at[d], rs.at[d], shifted(me, d, sign)
            ).start()
        return carry

    lax.fori_loop(0, 4, piece, 0)


def sent_round(me, src, dst, ss, rs, offsets):
    for d in offsets:
        remote(src.at[d], dst.at[d], ss.at[d], rs.at[d], me).wait_send()


def arrived_round(me, src, dst, ss, rs, offsets):
    for d in offsets:
        remote(src.at[d], dst.at[d], ss.at[d], rs.at[d], me).wait_recv()


STEP = {"y": 16, "z": 4, "x": 1}


def place_of(me, axis):
    return lax.rem(lax.div(me, STEP[axis]), 4)


def along(me, axis, delta):
    here = place_of(me, axis)
    there = lax.rem(here + delta, 4)
    return there, me + (there - here) * STEP[axis]


def order_of(me, order):
    first, second, third = (place_of(me, axis) for axis in order)
    return first * 16 + second * 4 + third


def chunks(rows):
    return [(r, min(BLOCK, rows)) for r in range(0, rows, BLOCK)]


def scatter_line(me, axis, src, dst, rows, send, recv, base, parts=None):
    for start, size in chunks(rows):
        if parts is not None and start // BLOCK not in parts:
            continue
        for delta in (1, 3, 2):
            there, target = along(me, axis, delta)
            remote(
                src.at[pl.ds(pl.multiple_of(there * rows + start, PIECE), size)],
                dst.at[delta, pl.ds(start, size)],
                send.at[base + delta], recv.at[base + delta], target,
            ).start()


def line_waits(me, ref, send, recv, base):
    return [
        remote(ref.at[delta], ref.at[delta], send.at[base + delta], recv.at[base + delta], me)
        for delta in range(1, 4)
    ]


def share_line(me, axis, full, first, rows, send, recv, base, parts=None):
    for start, size in chunks(rows):
        if parts is not None and start // BLOCK not in parts:
            continue
        for delta in (1, 3, 2):
            target = along(me, axis, delta)[1]
            ref = full.at[pl.ds(pl.multiple_of(first + start, PIECE), size)]
            remote(ref, ref, send.at[base + delta], recv.at[base + delta], target).start()


def share_waits(me, full, rows, send, recv, base):
    ref = full.at[pl.ds(0, rows)]
    return [
        remote(ref, ref, send.at[base + delta], recv.at[base + delta], me) for delta in range(1, 4)
    ]


def spread_order(order):
    return (order[2], PIECE), (order[1], 4 * PIECE), (order[0], QUART)


def first_row(me, order, rows):
    return pl.multiple_of(lax.div(order_of(me, order) * PIECE, rows) * rows, PIECE)


def fetch_kernel(
    glob, payload, k_ref, v_ref, cand_o, cand_l, recv, halo, gother, glast,
    ay, az, ax, gy, gz, ss, rs, hs, hr, us, ur, ls, lr, bs, br, own_sem,
):
    me = lax.axis_index("seq")
    enter(me)
    after = lax.rem(me + 1, SHARDS)
    before = lax.rem(me + SHARDS - 1, SHARDS)
    root = lax.div(glob[0] + glob[1] - (SHARDS * QB - 1), QB)

    def offset_of(axis):
        return lax.rem(place_of(me, axis) + 4 - place_of(root, axis), 4)

    own = pltpu.make_async_copy(payload.at[0], recv.at[0], own_sem)
    own.start()
    orders = ("yzx", "zyx")
    fulls = (gother, glast)
    mine = [pl.ds(first_row(me, order, PIECE), PIECE) for order in orders]

    @pl.when(me == LAST)
    def _():
        def scatter(t, carry):
            rows = pl.ds(first_row(t, "zyx", PIECE), PIECE)
            remote(cand_l.at[rows], glast.at[rows], ls.at[t], lr, t).start()
            return carry

        lax.fori_loop(0, LAST, scatter, 0)
        glast[mine[1], :] = cand_l[mine[1], :]

    def edge(part, far):
        for side, first, target, x in ((0, (QB - 1) * BLOCK, after, 3), (1, 0, before, 0)):

            @pl.when((place_of(me, "x") == x) == far)
            def _():
                for kv, ref in ((0, k_ref), (1, v_ref)):
                    remote(
                        ref.at[pl.ds(first + part * 16, 16)],
                        halo.at[side, kv, pl.ds(part * 16, 16)],
                        hs.at[2 * side + kv], hr.at[2 * side + kv], target,
                    ).start()

    halos = [
        remote(halo.at[n // 2, n % 2], halo.at[n // 2, n % 2], hs.at[n], hr.at[n], me)
        for n in range(4)
    ]
    ay[0] = cand_o[pl.ds(pl.multiple_of(place_of(me, "y") * QUART, QUART), QUART), :]
    up = [line_waits(me, ref, us, ur, 4 * n) for n, ref in enumerate((ay, az, ax))]
    down = [
        [
            share_waits(me, fulls[g], rows, bs, br, 12 * g + 4 * level)
            for level, (axis, rows) in enumerate(spread_order(orders[g]))
        ]
        for g in range(2)
    ]

    def share(g, level, parts=None):
        axis, rows = spread_order(orders[g])[level]
        share_line(
            me, axis, fulls[g], first_row(me, orders[g], rows), rows, bs, br, 12 * g + 4 * level,
            parts,
        )

    for part in range(4):
        scatter_line(me, "y", cand_o, ay, QUART, us, ur, 0, (part,))
        edge(part, False)
    later = []
    for number, offsets in enumerate(ROUNDS):
        if number >= DEPTH:
            sent_round(me, payload, recv, ss, rs, ROUNDS[number - DEPTH])
        for step in later:
            step()
        later = []
        send_round(me, 1, payload, recv, ss, rs, offsets)
        if number in FAR_AT:
            edge(FAR_AT.index(number), True)
        if number == FETCH_AT[0]:
            for copy in up[0]:
                copy.wait_recv()
            gy[...] = ay[offset_of("y")]
            later.append(lambda: scatter_line(me, "z", gy, az, 4 * PIECE, us, ur, 4))
            rows = pl.ds(pl.multiple_of(place_of(me, "z") * 4 * PIECE, 4 * PIECE), 4 * PIECE)
            az[0] = gy[rows, :]

            @pl.when(me != LAST)
            def _():
                remote(cand_l.at[mine[1]], glast.at[mine[1]], ls.at[0], lr, me).wait_recv()

            later.append(lambda: share(1, 0))
        if number == FETCH_AT[1]:
            for copy in up[1]:
                copy.wait_recv()
            gz[...] = az[offset_of("z")]
            later.append(lambda: scatter_line(me, "x", gz, ax, PIECE, us, ur, 8))
            ax[0] = gz[pl.ds(pl.multiple_of(place_of(me, "x") * PIECE, PIECE), PIECE), :]
            for copy in down[1][0]:
                copy.wait_recv()
            share(1, 1)
        if number == FETCH_AT[2]:
            for copy in up[2]:
                copy.wait_recv()
            gother[mine[0], :] = ax[offset_of("x")]
            later.append(lambda: share(0, 0))
            for copy in down[1][1]:
                copy.wait_recv()
        if number == FETCH_AT[3]:
            for copy in down[0][0]:
                copy.wait_recv()
            share(0, 1)
        if number == FETCH_AT[4]:
            for copy in down[0][1]:
                copy.wait_recv()
        if FETCH_AT[4] <= number < FETCH_AT[4] + 4:
            part = number - FETCH_AT[4]
            share(0, 2, (part,))
            share(1, 2, (part,))
            edge(part + 4, False)
    for offsets in ROUNDS[-DEPTH:]:
        sent_round(me, payload, recv, ss, rs, offsets)
    for offsets in ROUNDS:
        arrived_round(me, payload, recv, ss, rs, offsets)
    for line in up:
        for copy in line:
            copy.wait_send()
    for g in range(2):
        for level in range(3):
            for copy in down[g][level]:
                copy.wait_send()
                if level == 2:
                    copy.wait_recv()
    for copy in halos:
        copy.wait()

    @pl.when(me == LAST)
    def _():
        def done(t, carry):
            rows = pl.ds(first_row(t, "zyx", PIECE), PIECE)
            remote(cand_l.at[rows], glast.at[rows], ls.at[t], lr, t).wait_send()
            return carry

        lax.fori_loop(0, LAST, done, 0)

    own.wait()


def nt(a, b):
    return lax.dot_general(a, b, (((1,), (1,)), ((), ())), preferred_element_type=F32)


def nn(a, b):
    return lax.dot_general(a, b, (((1,), (0,)), ((), ())), preferred_element_type=F32)


def tn(a, b):
    return lax.dot_general(a, b, (((0,), (0,)), ((), ())), preferred_element_type=F32)


def attend_kernel(
    pick, q_ref, k_ref, v_ref, g_ref, halo_ref, other_ref, last_ref, recv,
    out_ref, dq_ref, center_ref, rim_ref, gpart_ref, outgoing,
    rk, rv, tk, tv, bandk, bandv, gk, gv, acck, accv, dsg, pgs, in_sem, out_sem,
):
    me = lax.axis_index("seq")
    h = pl.program_id(0)
    slot = lax.rem(h, 2)
    per_head = QB * RAND

    def load(head, buf):
        for e in range(per_head):
            s = pick[head * per_head + e]
            d, c = lax.div(s, 2), lax.rem(s, 2)
            rows = pl.ds(e * BLOCK, BLOCK)
            pltpu.make_async_copy(recv.at[d, c, 0], rk.at[buf, rows], in_sem.at[buf]).start()
            pltpu.make_async_copy(recv.at[d, c, 1], rv.at[buf, rows], in_sem.at[buf]).start()

    def drain(buf):
        pltpu.make_async_copy(tk.at[buf], tk.at[buf], out_sem.at[buf]).wait()
        pltpu.make_async_copy(tv.at[buf], tv.at[buf], out_sem.at[buf]).wait()

    @pl.when(h == 0)
    def _():
        load(0, 0)

    @pl.when(h + 1 < HEADS_HERE)
    def _():
        load(h + 1, 1 - slot)

    rows_here = QB * BLOCK
    for band, kv, ref in ((bandk, 0, k_ref), (bandv, 1, v_ref)):
        band[0:BLOCK] = halo_ref[0, kv]
        band[BLOCK : BLOCK + rows_here] = ref[...]
        band[BLOCK + rows_here :] = halo_ref[1, kv]
    for g, ref in ((0, other_ref), (1, last_ref)):
        gk[g * BLOCK : (g + 1) * BLOCK] = ref[0, 0]
        gv[g * BLOCK : (g + 1) * BLOCK] = ref[0, 1]
    acck[...] = jnp.zeros_like(acck)
    accv[...] = jnp.zeros_like(accv)
    pltpu.make_async_copy(rk.at[slot], rk.at[slot], in_sem.at[slot]).wait()
    pltpu.make_async_copy(rv.at[slot], rv.at[slot], in_sem.at[slot]).wait()

    @pl.when(h >= 2)
    def _():
        drain(slot)

    span = 3 * BLOCK
    col = lax.broadcasted_iota(jnp.int32, (BLOCK, span), 1)
    for i in range(QB):
        mine = slice(i * BLOCK, (i + 1) * BLOCK)
        q = q_ref[mine, :]
        g = g_ref[mine, :]
        wk, wv = bandk[i * BLOCK : i * BLOCK + span], bandv[i * BLOCK : i * BLOCK + span]
        ek, ev = rk[slot, i * span : (i + 1) * span], rv[slot, i * span : (i + 1) * span]
        sw = nt(q, wk) * SCALE
        if i == 0:
            sw = jnp.where((col < BLOCK) & (me == 0), MASKED, sw)
        if i == QB - 1:
            sw = jnp.where((col >= 2 * BLOCK) & (me == LAST), MASKED, sw)
        sr = nt(q, ek) * SCALE
        sg = nt(q, gk[...]) * SCALE
        peak = jnp.maximum(
            jnp.maximum(jnp.max(sw, axis=1, keepdims=True), jnp.max(sr, axis=1, keepdims=True)),
            jnp.max(sg, axis=1, keepdims=True),
        )
        sw, sr, sg = jnp.exp(sw - peak), jnp.exp(sr - peak), jnp.exp(sg - peak)
        total = (
            jnp.sum(sw, axis=1, keepdims=True)
            + jnp.sum(sr, axis=1, keepdims=True)
            + jnp.sum(sg, axis=1, keepdims=True)
        )
        inverse = 1.0 / total
        sw, sr, sg = sw * inverse, sr * inverse, sg * inverse
        pw, pr, pg = sw.astype(BF), sr.astype(BF), sg.astype(BF)
        out = (nn(pw, wv) + nn(pr, ev) + nn(pg, gv[...])).astype(BF)
        out_ref[mine, :] = out
        delta = jnp.sum(g.astype(F32) * out.astype(F32), axis=1, keepdims=True)
        dw = (sw * (nt(g, wv) - delta)).astype(BF)
        dr = (sr * (nt(g, ev) - delta)).astype(BF)
        dg = (sg * (nt(g, gv[...]) - delta)).astype(BF)
        dq_ref[mine, :] = ((nn(dw, wk) + nn(dr, ek) + nn(dg, gk[...])) * SCALE).astype(BF)
        acck[i * BLOCK : i * BLOCK + span] += tn(dw, q)
        accv[i * BLOCK : i * BLOCK + span] += tn(pw, g)
        tk[slot, i * span : (i + 1) * span] = (tn(dr, q) * SCALE).astype(BF)
        tv[slot, i * span : (i + 1) * span] = tn(pr, g).astype(BF)
        dsg[mine, :] = dg
        pgs[mine, :] = pg
    gdk = tn(dsg[...], q_ref[...]) * SCALE
    gdv = tn(pgs[...], g_ref[...])
    for g in range(2):
        gpart_ref[g, 0, 0] = gdk[g * BLOCK : (g + 1) * BLOCK].astype(BF)
        gpart_ref[g, 0, 1] = gdv[g * BLOCK : (g + 1) * BLOCK].astype(BF)
    center_ref[0] = acck[BLOCK : BLOCK + rows_here] * SCALE
    center_ref[1] = accv[BLOCK : BLOCK + rows_here]
    rim_ref[0, 0] = (acck[0:BLOCK] * SCALE).astype(BF)
    rim_ref[0, 1] = accv[0:BLOCK].astype(BF)
    rim_ref[1, 0] = (acck[BLOCK + rows_here :] * SCALE).astype(BF)
    rim_ref[1, 1] = accv[BLOCK + rows_here :].astype(BF)
    for e in range(per_head):
        s = pick[h * per_head + e]
        d, c = lax.div(s, 2), lax.rem(s, 2)
        rows = pl.ds(e * BLOCK, BLOCK)
        pltpu.make_async_copy(tk.at[slot, rows], outgoing.at[d, c, 0], out_sem.at[slot]).start()
        pltpu.make_async_copy(tv.at[slot, rows], outgoing.at[d, c, 1], out_sem.at[slot]).start()

    @pl.when(h == HEADS_HERE - 1)
    def _():
        drain(1 - slot)
        drain(slot)


def return_kernel(
    outgoing, rim, gpart, returned, rim_back, gother, glast,
    ra, rb, rc, pa, pb, pc, ss, rs, hs, hr, us, ur, ls, lr, bs, br, own_sem,
):
    me = lax.axis_index("seq")
    enter(me)
    after = lax.rem(me + 1, SHARDS)
    before = lax.rem(me + SHARDS - 1, SHARDS)
    own = pltpu.make_async_copy(outgoing.at[0], returned.at[0], own_sem)
    own.start()
    orders = ("yzx", "zyx")
    mine = [pl.ds(first_row(me, order, PIECE), PIECE) for order in orders]
    stages = ((ra, QUART), (rb, 4 * PIECE), (rc, PIECE))
    sums = (pa, pb, pc)

    def reduce_start(g, level, parts=None):
        src = gpart.at[g] if level == 0 else sums[level - 1].at[g]
        dst, rows = stages[level]
        scatter_line(
            me, orders[g][level], src, dst.at[g], rows, us, ur, 12 * g + 4 * level, parts
        )

    def reduce_finish(g, level):
        src = gpart.at[g] if level == 0 else sums[level - 1].at[g]
        dst, rows = stages[level]
        for copy in waits[g][level]:
            copy.wait_recv()
        here = pl.multiple_of(place_of(me, orders[g][level]) * rows, rows)
        total = src[pl.ds(here, rows), :].astype(F32)
        for delta in range(1, 4):
            total = total + dst[g, delta].astype(F32)
        sums[level][g] = total.astype(BF)

    waits = [
        [line_waits(me, ref.at[g], us, ur, 12 * g + 4 * n) for n, (ref, _) in enumerate(stages)]
        for g in range(2)
    ]
    def edge(part, far):
        rows = pl.ds(part * 16, 16)
        for side, target, x in ((0, before, 0), (1, after, 3)):

            @pl.when((place_of(me, "x") == x) == far)
            def _():
                for kv in range(2):
                    remote(
                        rim.at[side, kv, rows], rim_back.at[1 - side, kv, rows],
                        hs.at[2 * side + kv], hr.at[2 * side + kv], target,
                    ).start()

    halos = [
        remote(rim.at[n // 2, n % 2], rim_back.at[n // 2, n % 2], hs.at[n], hr.at[n], me)
        for n in range(4)
    ]
    levels = spread_order(orders[0])
    down = [
        share_waits(me, gother, rows, bs, br, 4 * level) for level, (_, rows) in enumerate(levels)
    ]

    def share(level, parts=None):
        axis, rows = levels[level]
        first = first_row(me, orders[0], rows)
        share_line(me, axis, gother, first, rows, bs, br, 4 * level, parts)

    for part in range(4):
        for g in range(2):
            reduce_start(g, 0, (part,))
        edge(part, False)
    later = []
    for number, offsets in enumerate(ROUNDS):
        if number >= DEPTH:
            sent_round(me, outgoing, returned, ss, rs, ROUNDS[number - DEPTH])
        for step in later:
            step()
        later = []
        send_round(me, -1, outgoing, returned, ss, rs, offsets)
        if number in FAR_AT:
            edge(FAR_AT.index(number), True)
        if number == RETURN_AT[0]:
            for g in range(2):
                reduce_finish(g, 0)
                later.append(functools.partial(reduce_start, g, 1))
        if number == RETURN_AT[1]:
            for g in range(2):
                reduce_finish(g, 1)
                later.append(functools.partial(reduce_start, g, 2))
        if number == RETURN_AT[2]:
            for g in range(2):
                reduce_finish(g, 2)
            gother[mine[0], :] = pc[0]

            def pass_on():
                share(0)

                @pl.when(me != LAST)
                def _():
                    remote(pc.at[1], glast.at[mine[1]], ls, lr.at[me], LAST).start()

            later.append(pass_on)

            @pl.when(me == LAST)
            def _():
                glast[mine[1], :] = pc[1]

        if number == RETURN_AT[3]:
            for copy in down[0]:
                copy.wait_recv()
            share(1)
        if number == RETURN_AT[4]:
            for copy in down[1]:
                copy.wait_recv()
        if RETURN_AT[4] <= number < RETURN_AT[4] + 4:
            part = number - RETURN_AT[4]
            share(2, (part,))
            edge(part + 4, False)
    for offsets in ROUNDS[-DEPTH:]:
        sent_round(me, outgoing, returned, ss, rs, offsets)
    for offsets in ROUNDS:
        arrived_round(me, outgoing, returned, ss, rs, offsets)
    for g in range(2):
        for line in waits[g]:
            for copy in line:
                copy.wait_send()
    for level in range(3):
        for copy in down[level]:
            copy.wait_send()
            if level == 2:
                copy.wait_recv()
    for copy in halos:
        copy.wait()

    @pl.when(me != LAST)
    def _():
        remote(pc.at[1], glast.at[mine[1]], ls, lr.at[me], LAST).wait_send()

    @pl.when(me == LAST)
    def _():
        def done(t, carry):
            rows = pl.ds(first_row(t, "zyx", PIECE), PIECE)
            remote(pc.at[1], glast.at[rows], ls, lr.at[t], t).wait_recv()
            return carry

        lax.fori_loop(0, LAST, done, 0)

    own.wait()


CHUNK = 4


def collect_kernel(
    glob, codes, center, rim, gother, glast, returned, dk_ref, dv_ref, buf, acc, sem, csem
):
    me = lax.axis_index("seq")
    steps = SHARDS // CHUNK

    def fetch(step):
        place = pl.ds(pl.multiple_of(step * CHUNK, CHUNK), CHUNK)
        return pltpu.make_async_copy(returned.at[place], buf.at[place], sem.at[step])

    whole = pltpu.make_async_copy(center, acc, csem)
    whole.start()
    for step in range(steps):
        fetch(step).start()
    whole.wait()
    for kv in range(2):
        acc[kv, 0:BLOCK, :] += rim[0, kv].astype(F32)
        acc[kv, (QB - 1) * BLOCK :, :] += rim[1, kv].astype(F32)

    def add_glob(blk, ref):
        rows = pl.ds(pl.multiple_of(blk * BLOCK, BLOCK), BLOCK)
        for h in range(HEADS_HERE):
            for kv in range(2):
                src = ref[pl.ds((2 * h + kv) * BLOCK, BLOCK), :]
                acc[kv, rows, pl.ds(h * DH, DH)] += src.astype(F32)

    @pl.when(me == LAST)
    def _():
        add_glob(QB - 1, glast)

    other = glob[0] + glob[1] - (SHARDS * QB - 1)

    @pl.when(me == lax.div(other, QB))
    def _():
        add_glob(lax.rem(other, QB), gother)

    def add(code, d, c):
        head = lax.div(code, 4 * QB * RAND)
        blk = lax.rem(code, 4)
        rows = pl.ds(pl.multiple_of(blk * BLOCK, BLOCK), BLOCK)
        cols = pl.ds(pl.multiple_of(head * DH, DH), DH)
        for kv in range(2):
            acc[kv, rows, cols] += buf[d, c, kv].astype(F32)

    def step_body(step, carry):
        fetch(step).wait()
        for place in range(CHUNK):
            d = step * CHUNK + place
            t = moved(me, d)
            low, high = codes[0, t], codes[1, t]

            @pl.when(low < NONE)
            def _():
                add(low, d, 0)

            @pl.when(high > low)
            def _():
                add(high, d, 1)

        return carry

    lax.fori_loop(0, steps, step_body, 0)
    dk_ref[...] = acc[0].astype(BF)
    dv_ref[...] = acc[1].astype(BF)


def smem():
    return pl.BlockSpec(memory_space=pltpu.SMEM)


def vmem():
    return pl.BlockSpec(memory_space=pltpu.VMEM)


def hbm():
    return pl.BlockSpec(memory_space=ANY)


def dma(*shape):
    return pltpu.SemaphoreType.DMA(shape)


def body(queries, keys, values, out_grad, rand_ids, glob_ids):
    place = lax.axis_index("seq")
    group = lax.axis_index("head")
    shape = jax.ShapeDtypeStruct
    ids = lax.dynamic_slice_in_dim(rand_ids, group * HEADS_HERE, HEADS_HERE, 0)
    ids = ids.reshape(HEADS_HERE, SHARDS, QB * RAND)
    own_ids = lax.dynamic_index_in_dim(ids, place, 1, False).reshape(ENTRIES)
    table = ids.transpose(0, 2, 1).reshape(ENTRIES, SHARDS)
    slots = shape((SHARDS, 2, 2, BLOCK, DH), BF)
    grows = shape((GROWS, DH), BF)
    width = HEADS_HERE * DH
    rows_here = QB * BLOCK

    payload, cand_o, cand_l, pick, codes = pl.pallas_call(
        prep_kernel,
        out_shape=(
            slots, grows, grows, shape((ENTRIES,), jnp.int32), shape((2, SHARDS), jnp.int32)
        ),
        in_specs=[smem(), smem(), vmem(), vmem(), vmem()],
        out_specs=(hbm(), hbm(), hbm(), smem(), vmem()),
        scratch_shapes=[
            pltpu.SMEM((SHARDS,), jnp.int32),
            pltpu.SMEM((2, SHARDS), jnp.int32),
            pltpu.SemaphoreType.DMA, dma(2), pltpu.SemaphoreType.DMA,
        ],
        name="prep",
    )(glob_ids, own_ids, table, keys, values)

    recv, halo, gother, glast = pl.pallas_call(
        fetch_kernel,
        out_shape=(slots, shape((2, 2, BLOCK, width), BF), grows, grows),
        in_specs=[smem(), hbm(), hbm(), hbm(), vmem(), vmem()],
        out_specs=(hbm(), hbm(), vmem(), vmem()),
        scratch_shapes=[
            pltpu.VMEM((4, QUART, DH), BF),
            pltpu.VMEM((4, 4 * PIECE, DH), BF),
            pltpu.VMEM((4, PIECE, DH), BF),
            pltpu.VMEM((QUART, DH), BF),
            pltpu.VMEM((4 * PIECE, DH), BF),
            dma(SHARDS), dma(SHARDS), dma(4), dma(4), dma(12), dma(12),
            dma(SHARDS), pltpu.SemaphoreType.DMA, dma(24), dma(24), pltpu.SemaphoreType.DMA,
        ],
        compiler_params=pltpu.CompilerParams(collective_id=0, has_side_effects=True),
        name="fetch",
    )(glob_ids, payload, keys, values, cand_o, cand_l)

    span = 3 * BLOCK
    head_block = pl.BlockSpec((rows_here, DH), lambda h, *_: (0, h))
    side_block = pl.BlockSpec((2, 2, BLOCK, DH), lambda h, *_: (0, 0, 0, h))
    one_block = pl.BlockSpec((1, 2, BLOCK, DH), lambda h, *_: (h, 0, 0, 0))
    glob_block = pl.BlockSpec((2, 1, 2, BLOCK, DH), lambda h, *_: (0, h, 0, 0, 0))
    full = QB * span
    out, dq, center, rim, gpart, outgoing = pl.pallas_call(
        attend_kernel,
        out_shape=(
            shape((rows_here, width), BF),
            shape((rows_here, width), BF),
            shape((2, rows_here, width), F32),
            shape((2, 2, BLOCK, width), BF),
            shape((2, HEADS_HERE, 2, BLOCK, DH), BF),
            slots,
        ),
        grid_spec=pltpu.PrefetchScalarGridSpec(
            num_scalar_prefetch=1,
            grid=(HEADS_HERE,),
            in_specs=[head_block] * 4 + [side_block, one_block, one_block, hbm()],
            out_specs=[
                head_block,
                head_block,
                pl.BlockSpec((2, rows_here, DH), lambda h, *_: (0, 0, h)),
                side_block,
                glob_block,
                hbm(),
            ],
            scratch_shapes=[pltpu.VMEM((2, full, DH), BF)] * 4
            + [pltpu.VMEM((rows_here + 2 * BLOCK, DH), BF)] * 2
            + [pltpu.VMEM((2 * BLOCK, DH), BF)] * 2
            + [pltpu.VMEM((rows_here + 2 * BLOCK, DH), F32)] * 2
            + [pltpu.VMEM((rows_here, 2 * BLOCK), BF)] * 2
            + [dma(2), dma(2)],
        ),
        name="attend",
    )(
        pick, queries, keys, values, out_grad, halo,
        gother.reshape(HEADS_HERE, 2, BLOCK, DH), glast.reshape(HEADS_HERE, 2, BLOCK, DH), recv,
    )

    returned, rim_back, sum_other, sum_last = pl.pallas_call(
        return_kernel,
        out_shape=(slots, shape((2, 2, BLOCK, width), BF), grows, grows),
        in_specs=[hbm(), hbm(), vmem()],
        out_specs=(hbm(), hbm(), vmem(), vmem()),
        scratch_shapes=[
            pltpu.VMEM((2, 4, QUART, DH), BF),
            pltpu.VMEM((2, 4, 4 * PIECE, DH), BF),
            pltpu.VMEM((2, 4, PIECE, DH), BF),
            pltpu.VMEM((2, QUART, DH), BF),
            pltpu.VMEM((2, 4 * PIECE, DH), BF),
            pltpu.VMEM((2, PIECE, DH), BF),
            dma(SHARDS), dma(SHARDS), dma(4), dma(4), dma(24), dma(24),
            pltpu.SemaphoreType.DMA, dma(SHARDS), dma(12), dma(12), pltpu.SemaphoreType.DMA,
        ],
        compiler_params=pltpu.CompilerParams(collective_id=1, has_side_effects=True),
        name="return",
    )(outgoing, rim, gpart.reshape(2, GROWS, DH))

    dk, dv = pl.pallas_call(
        collect_kernel,
        out_shape=(shape((rows_here, width), BF), shape((rows_here, width), BF)),
        in_specs=[smem(), smem(), hbm(), vmem(), vmem(), vmem(), hbm()],
        out_specs=(vmem(), vmem()),
        scratch_shapes=[
            pltpu.VMEM((SHARDS, 2, 2, BLOCK, DH), BF),
            pltpu.VMEM((2, rows_here, width), F32),
            dma(SHARDS // CHUNK),
            pltpu.SemaphoreType.DMA,
        ],
        name="collect",
    )(glob_ids, codes, center, rim_back, sum_other, sum_last, returned)
    return out, dq, dk, dv


def solution(mesh):
    rows = P("seq", "head")
    return jax.shard_map(
        body,
        mesh=mesh,
        in_specs=(rows, rows, rows, rows, P(), P()),
        out_specs=(rows, rows, rows, rows),
        check_vma=False,
    )
```

```python
import functools
import math

import jax
import jax.numpy as jnp
from jax import lax
from jax.experimental import pallas as pl
from jax.experimental.pallas import tpu as pltpu
from jax.sharding import PartitionSpec as P

BLOCK = 128
DH = 128
RAND = 3
HEADS_HERE = 8
QB = 4
SHARDS = 64
ENTRIES = HEADS_HERE * QB * RAND
NONE = 1 << 20
DEPTH = 6
FETCH_AT = (1, 3, 5, 8, 9)
FETCH_FAR = (0, 1, 2, 3, 5, 6, 9, 11)
RETURN_FAR = (1, 2, 3, 4, 5, 6, 7, 8)
RETURN_AT = (3, 4, 5, 6, 7)
LAST = SHARDS - 1
GROWS = HEADS_HERE * 2 * BLOCK
PIECE = GROWS // SHARDS
QUART = GROWS // 4
SCALE = 1.0 / math.sqrt(DH)
MASKED = -1e30
MESH = pl.DeviceIdType.MESH
ANY = pl.ANY
BF = jnp.bfloat16
F32 = jnp.float32


def orbits():
    def key(d):
        return (d // 16, (d // 4) % 4, d % 4)

    def hops(d):
        return sum(min(v, 4 - v) for v in key(d))

    seen, rounds = set(), []
    for d in sorted(range(1, SHARDS), key=lambda d: (hops(d), d)):
        if d in seen:
            continue
        orbit = []
        for turn in range(3):
            k = key(d)[turn:] + key(d)[:turn]
            for sign in (1, -1):
                a, b, c = ((sign * v) % 4 for v in k)
                if a * 16 + b * 4 + c not in orbit:
                    orbit.append(a * 16 + b * 4 + c)
        seen.update(orbit)
        rounds.append(orbit)
    return rounds


ROUNDS = orbits()


def moved(me, d, sign=1):
    y, z, x = lax.div(me, 16), lax.rem(lax.div(me, 4), 4), lax.rem(me, 4)
    dy, dz, dx = lax.div(d, 16), lax.rem(lax.div(d, 4), 4), lax.rem(d, 4)
    if sign < 0:
        dy, dz, dx = 4 - dy, 4 - dz, 4 - dx
    return lax.rem(y + dy, 4) * 16 + lax.rem(z + dz, 4) * 4 + lax.rem(x + dx, 4)


def shifted(me, d, sign=1):
    dy, dz, dx = d // 16, (d // 4) % 4, d % 4
    if sign < 0:
        dy, dz, dx = 4 - dy, 4 - dz, 4 - dx
    y, z, x = lax.div(me, 16), lax.rem(lax.div(me, 4), 4), lax.rem(me, 4)
    return lax.rem(y + dy, 4) * 16 + lax.rem(z + dz, 4) * 4 + lax.rem(x + dx, 4)


def remote(src, dst, send, recv, target):
    return pltpu.make_async_remote_copy(
        src_ref=src,
        dst_ref=dst,
        send_sem=send,
        recv_sem=recv,
        device_id={"seq": target},
        device_id_type=MESH,
    )


def enter(me):
    barrier = pltpu.get_barrier_semaphore()

    def greet(d, carry):
        pl.semaphore_signal(
            barrier, inc=1, device_id={"seq": moved(me, d)}, device_id_type=MESH
        )
        return carry

    lax.fori_loop(1, SHARDS, greet, 0)
    pl.semaphore_wait(barrier, SHARDS - 1)


def prep_kernel(
    glob, own_ids, ids, k_ref, v_ref, payload, cand_o, cand_l, pick, codes, count, table, sem,
    gsem, tsem,
):
    me = lax.axis_index("seq")
    entry = lax.broadcasted_iota(jnp.int32, (ENTRIES, SHARDS), 0)
    code = entry * 4 + (ids[...] & 3)
    hit = (ids[...] >> 2) == me
    codes[0:1, :] = jnp.min(jnp.where(hit, code, NONE), axis=0, keepdims=True)
    codes[1:2, :] = jnp.max(jnp.where(hit, code, -1), axis=0, keepdims=True)
    to_scalar = pltpu.make_async_copy(codes, table, tsem)
    to_scalar.start()
    other = glob[0] + glob[1] - (SHARDS * QB - 1)
    rows_o = pl.ds(pl.multiple_of(lax.rem(other, QB) * BLOCK, BLOCK), BLOCK)
    rows_l = pl.ds((QB - 1) * BLOCK, BLOCK)
    for h in range(HEADS_HERE):
        cols = pl.ds(h * DH, DH)
        for kv, ref in ((0, k_ref), (1, v_ref)):
            dst = pl.ds((2 * h + kv) * BLOCK, BLOCK)
            pltpu.make_async_copy(ref.at[rows_o, cols], cand_o.at[dst], gsem.at[0]).start()
            pltpu.make_async_copy(ref.at[rows_l, cols], cand_l.at[dst], gsem.at[1]).start()
    to_scalar.wait()

    def put(d, carry):
        t = moved(me, d)
        low = table[0, t]
        high = table[1, t]
        count[t] = 0
        for c, code in ((0, jnp.where(low < NONE, low, 0)), (1, jnp.maximum(high, 0))):
            head = lax.div(code, 4 * QB * RAND)
            blk = lax.rem(code, 4)
            rows = pl.ds(pl.multiple_of(blk * BLOCK, BLOCK), BLOCK)
            cols = pl.ds(pl.multiple_of(head * DH, DH), DH)
            pltpu.make_async_copy(k_ref.at[rows, cols], payload.at[d, c, 0], sem).start()
            pltpu.make_async_copy(v_ref.at[rows, cols], payload.at[d, c, 1], sem).start()
        return carry

    lax.fori_loop(0, SHARDS, put, 0)

    def choose(e, carry):
        src = lax.div(own_ids[e], 4)
        seen = count[src]
        count[src] = seen + 1
        away = 0
        for axis in "yzx":
            gap = lax.rem(place_of(me, axis) + 4 - place_of(src, axis), 4)
            away = away + gap * STEP[axis]
        pick[e] = away * 2 + jnp.minimum(seen, 1)
        return carry

    lax.fori_loop(0, ENTRIES, choose, 0)
    pltpu.make_async_copy(cand_o, cand_o, gsem.at[0]).wait()
    pltpu.make_async_copy(cand_l, cand_l, gsem.at[1]).wait()
    pltpu.make_async_copy(payload, payload, sem).wait()


def send_round(me, sign, src, dst, ss, rs, offsets):
    def piece(i, carry):
        c, kv = lax.div(i, 2), lax.rem(i, 2)
        for d in offsets:
            remote(
                src.at[d, c, kv], dst.at[d, c, kv], ss.at[d], rs.at[d], shifted(me, d, sign)
            ).start()
        return carry

    lax.fori_loop(0, 4, piece, 0)


def sent_round(me, src, dst, ss, rs, offsets):
    for d in offsets:
        remote(src.at[d], dst.at[d], ss.at[d], rs.at[d], me).wait_send()


def arrived_round(me, src, dst, ss, rs, offsets):
    for d in offsets:
        remote(src.at[d], dst.at[d], ss.at[d], rs.at[d], me).wait_recv()


STEP = {"y": 16, "z": 4, "x": 1}


def place_of(me, axis):
    return lax.rem(lax.div(me, STEP[axis]), 4)


def along(me, axis, delta):
    here = place_of(me, axis)
    there = lax.rem(here + delta, 4)
    return there, me + (there - here) * STEP[axis]


def order_of(me, order):
    first, second, third = (place_of(me, axis) for axis in order)
    return first * 16 + second * 4 + third


def chunks(rows):
    return [(r, min(BLOCK, rows)) for r in range(0, rows, BLOCK)]


def scatter_line(me, axis, src, dst, rows, send, recv, base, parts=None):
    for start, size in chunks(rows):
        if parts is not None and start // BLOCK not in parts:
            continue
        for delta in (1, 3, 2):
            there, target = along(me, axis, delta)
            remote(
                src.at[pl.ds(pl.multiple_of(there * rows + start, PIECE), size)],
                dst.at[delta, pl.ds(start, size)],
                send.at[base + delta], recv.at[base + delta], target,
            ).start()


def line_waits(me, ref, send, recv, base):
    return [
        remote(ref.at[delta], ref.at[delta], send.at[base + delta], recv.at[base + delta], me)
        for delta in range(1, 4)
    ]


def share_line(me, axis, full, first, rows, send, recv, base, parts=None):
    for start, size in chunks(rows):
        if parts is not None and start // BLOCK not in parts:
            continue
        for delta in (1, 3, 2):
            target = along(me, axis, delta)[1]
            ref = full.at[pl.ds(pl.multiple_of(first + start, PIECE), size)]
            remote(ref, ref, send.at[base + delta], recv.at[base + delta], target).start()


def share_waits(me, full, rows, send, recv, base):
    ref = full.at[pl.ds(0, rows)]
    return [
        remote(ref, ref, send.at[base + delta], recv.at[base + delta], me) for delta in range(1, 4)
    ]


def spread_order(order):
    return (order[2], PIECE), (order[1], 4 * PIECE), (order[0], QUART)


def first_row(me, order, rows):
    return pl.multiple_of(lax.div(order_of(me, order) * PIECE, rows) * rows, PIECE)


def fetch_kernel(
    glob, payload, k_ref, v_ref, cand_o, cand_l, recv, halo, gother, glast,
    ay, az, ax, gy, gz, ss, rs, hs, hr, us, ur, ls, lr, bs, br, own_sem,
):
    me = lax.axis_index("seq")
    enter(me)
    after = lax.rem(me + 1, SHARDS)
    before = lax.rem(me + SHARDS - 1, SHARDS)
    root = lax.div(glob[0] + glob[1] - (SHARDS * QB - 1), QB)

    def offset_of(axis):
        return lax.rem(place_of(me, axis) + 4 - place_of(root, axis), 4)

    own = pltpu.make_async_copy(payload.at[0], recv.at[0], own_sem)
    own.start()
    orders = ("yzx", "zyx")
    fulls = (gother, glast)
    mine = [pl.ds(first_row(me, order, PIECE), PIECE) for order in orders]

    @pl.when(me == LAST)
    def _():
        def scatter(t, carry):
            rows = pl.ds(first_row(t, "zyx", PIECE), PIECE)
            remote(cand_l.at[rows], glast.at[rows], ls.at[t], lr, t).start()
            return carry

        lax.fori_loop(0, LAST, scatter, 0)
        glast[mine[1], :] = cand_l[mine[1], :]

    def edge(part, far):
        for side, first, target, x in ((0, (QB - 1) * BLOCK, after, 3), (1, 0, before, 0)):

            @pl.when((place_of(me, "x") == x) == far)
            def _():
                for kv, ref in ((0, k_ref), (1, v_ref)):
                    remote(
                        ref.at[pl.ds(first + part * 16, 16)],
                        halo.at[side, kv, pl.ds(part * 16, 16)],
                        hs.at[2 * side + kv], hr.at[2 * side + kv], target,
                    ).start()

    halos = [
        remote(halo.at[n // 2, n % 2], halo.at[n // 2, n % 2], hs.at[n], hr.at[n], me)
        for n in range(4)
    ]
    ay[0] = cand_o[pl.ds(pl.multiple_of(place_of(me, "y") * QUART, QUART), QUART), :]
    up = [line_waits(me, ref, us, ur, 4 * n) for n, ref in enumerate((ay, az, ax))]
    down = [
        [
            share_waits(me, fulls[g], rows, bs, br, 12 * g + 4 * level)
            for level, (axis, rows) in enumerate(spread_order(orders[g]))
        ]
        for g in range(2)
    ]

    def share(g, level, parts=None):
        axis, rows = spread_order(orders[g])[level]
        share_line(
            me, axis, fulls[g], first_row(me, orders[g], rows), rows, bs, br, 12 * g + 4 * level,
            parts,
        )

    for part in range(4):
        scatter_line(me, "y", cand_o, ay, QUART, us, ur, 0, (part,))
        edge(part, False)
    later = []
    for number, offsets in enumerate(ROUNDS):
        if number >= DEPTH:
            sent_round(me, payload, recv, ss, rs, ROUNDS[number - DEPTH])
        for step in later:
            step()
        later = []
        send_round(me, 1, payload, recv, ss, rs, offsets)
        if number in FETCH_FAR:
            edge(FETCH_FAR.index(number), True)
        if number == FETCH_AT[0]:
            for copy in up[0]:
                copy.wait_recv()
            gy[...] = ay[offset_of("y")]
            later.append(lambda: scatter_line(me, "z", gy, az, 4 * PIECE, us, ur, 4))
            rows = pl.ds(pl.multiple_of(place_of(me, "z") * 4 * PIECE, 4 * PIECE), 4 * PIECE)
            az[0] = gy[rows, :]

            @pl.when(me != LAST)
            def _():
                remote(cand_l.at[mine[1]], glast.at[mine[1]], ls.at[0], lr, me).wait_recv()

            later.append(lambda: share(1, 0))
        if number == FETCH_AT[1]:
            for copy in up[1]:
                copy.wait_recv()
            gz[...] = az[offset_of("z")]
            later.append(lambda: scatter_line(me, "x", gz, ax, PIECE, us, ur, 8))
            ax[0] = gz[pl.ds(pl.multiple_of(place_of(me, "x") * PIECE, PIECE), PIECE), :]
            for copy in down[1][0]:
                copy.wait_recv()
            share(1, 1)
        if number == FETCH_AT[2]:
            for copy in up[2]:
                copy.wait_recv()
            gother[mine[0], :] = ax[offset_of("x")]
            later.append(lambda: share(0, 0))
            for copy in down[1][1]:
                copy.wait_recv()
        if number == FETCH_AT[3]:
            for copy in down[0][0]:
                copy.wait_recv()
            share(0, 1)
        if number == FETCH_AT[4]:
            for copy in down[0][1]:
                copy.wait_recv()
        if FETCH_AT[4] <= number < FETCH_AT[4] + 4:
            part = number - FETCH_AT[4]
            share(0, 2, (part,))
            share(1, 2, (part,))
            edge(part + 4, False)
    for offsets in ROUNDS[-DEPTH:]:
        sent_round(me, payload, recv, ss, rs, offsets)
    for offsets in ROUNDS:
        arrived_round(me, payload, recv, ss, rs, offsets)
    for line in up:
        for copy in line:
            copy.wait_send()
    for g in range(2):
        for level in range(3):
            for copy in down[g][level]:
                copy.wait_send()
                if level == 2:
                    copy.wait_recv()
    for copy in halos:
        copy.wait()

    @pl.when(me == LAST)
    def _():
        def done(t, carry):
            rows = pl.ds(first_row(t, "zyx", PIECE), PIECE)
            remote(cand_l.at[rows], glast.at[rows], ls.at[t], lr, t).wait_send()
            return carry

        lax.fori_loop(0, LAST, done, 0)

    own.wait()


def nt(a, b):
    return lax.dot_general(a, b, (((1,), (1,)), ((), ())), preferred_element_type=F32)


def nn(a, b):
    return lax.dot_general(a, b, (((1,), (0,)), ((), ())), preferred_element_type=F32)


def tn(a, b):
    return lax.dot_general(a, b, (((0,), (0,)), ((), ())), preferred_element_type=F32)


def attend_kernel(
    pick, q_ref, k_ref, v_ref, g_ref, halo_ref, other_ref, last_ref, recv,
    out_ref, dq_ref, center_ref, rim_ref, gpart_ref, outgoing,
    rk, rv, tk, tv, bandk, bandv, gk, gv, acck, accv, dsg, pgs, in_sem, out_sem,
):
    me = lax.axis_index("seq")
    h = pl.program_id(0)
    slot = lax.rem(h, 2)
    per_head = QB * RAND

    def load(head, buf):
        for e in range(per_head):
            s = pick[head * per_head + e]
            d, c = lax.div(s, 2), lax.rem(s, 2)
            rows = pl.ds(e * BLOCK, BLOCK)
            pltpu.make_async_copy(recv.at[d, c, 0], rk.at[buf, rows], in_sem.at[buf]).start()
            pltpu.make_async_copy(recv.at[d, c, 1], rv.at[buf, rows], in_sem.at[buf]).start()

    def drain(buf):
        pltpu.make_async_copy(tk.at[buf], tk.at[buf], out_sem.at[buf]).wait()
        pltpu.make_async_copy(tv.at[buf], tv.at[buf], out_sem.at[buf]).wait()

    @pl.when(h == 0)
    def _():
        load(0, 0)

    @pl.when(h + 1 < HEADS_HERE)
    def _():
        load(h + 1, 1 - slot)

    rows_here = QB * BLOCK
    for band, kv, ref in ((bandk, 0, k_ref), (bandv, 1, v_ref)):
        band[0:BLOCK] = halo_ref[0, kv]
        band[BLOCK : BLOCK + rows_here] = ref[...]
        band[BLOCK + rows_here :] = halo_ref[1, kv]
    for g, ref in ((0, other_ref), (1, last_ref)):
        gk[g * BLOCK : (g + 1) * BLOCK] = ref[0, 0]
        gv[g * BLOCK : (g + 1) * BLOCK] = ref[0, 1]
    acck[...] = jnp.zeros_like(acck)
    accv[...] = jnp.zeros_like(accv)
    pltpu.make_async_copy(rk.at[slot], rk.at[slot], in_sem.at[slot]).wait()
    pltpu.make_async_copy(rv.at[slot], rv.at[slot], in_sem.at[slot]).wait()

    @pl.when(h >= 2)
    def _():
        drain(slot)

    span = 3 * BLOCK
    col = lax.broadcasted_iota(jnp.int32, (BLOCK, span), 1)
    for i in range(QB):
        mine = slice(i * BLOCK, (i + 1) * BLOCK)
        q = q_ref[mine, :]
        g = g_ref[mine, :]
        wk, wv = bandk[i * BLOCK : i * BLOCK + span], bandv[i * BLOCK : i * BLOCK + span]
        ek, ev = rk[slot, i * span : (i + 1) * span], rv[slot, i * span : (i + 1) * span]
        sw = nt(q, wk) * SCALE
        if i == 0:
            sw = jnp.where((col < BLOCK) & (me == 0), MASKED, sw)
        if i == QB - 1:
            sw = jnp.where((col >= 2 * BLOCK) & (me == LAST), MASKED, sw)
        sr = nt(q, ek) * SCALE
        sg = nt(q, gk[...]) * SCALE
        peak = jnp.maximum(
            jnp.maximum(jnp.max(sw, axis=1, keepdims=True), jnp.max(sr, axis=1, keepdims=True)),
            jnp.max(sg, axis=1, keepdims=True),
        )
        sw, sr, sg = jnp.exp(sw - peak), jnp.exp(sr - peak), jnp.exp(sg - peak)
        total = (
            jnp.sum(sw, axis=1, keepdims=True)
            + jnp.sum(sr, axis=1, keepdims=True)
            + jnp.sum(sg, axis=1, keepdims=True)
        )
        inverse = 1.0 / total
        sw, sr, sg = sw * inverse, sr * inverse, sg * inverse
        pw, pr, pg = sw.astype(BF), sr.astype(BF), sg.astype(BF)
        out = (nn(pw, wv) + nn(pr, ev) + nn(pg, gv[...])).astype(BF)
        out_ref[mine, :] = out
        delta = jnp.sum(g.astype(F32) * out.astype(F32), axis=1, keepdims=True)
        dw = (sw * (nt(g, wv) - delta)).astype(BF)
        dr = (sr * (nt(g, ev) - delta)).astype(BF)
        dg = (sg * (nt(g, gv[...]) - delta)).astype(BF)
        dq_ref[mine, :] = ((nn(dw, wk) + nn(dr, ek) + nn(dg, gk[...])) * SCALE).astype(BF)
        acck[i * BLOCK : i * BLOCK + span] += tn(dw, q)
        accv[i * BLOCK : i * BLOCK + span] += tn(pw, g)
        tk[slot, i * span : (i + 1) * span] = (tn(dr, q) * SCALE).astype(BF)
        tv[slot, i * span : (i + 1) * span] = tn(pr, g).astype(BF)
        dsg[mine, :] = dg
        pgs[mine, :] = pg
    gdk = tn(dsg[...], q_ref[...]) * SCALE
    gdv = tn(pgs[...], g_ref[...])
    for g in range(2):
        gpart_ref[g, 0, 0] = gdk[g * BLOCK : (g + 1) * BLOCK].astype(BF)
        gpart_ref[g, 0, 1] = gdv[g * BLOCK : (g + 1) * BLOCK].astype(BF)
    center_ref[0] = acck[BLOCK : BLOCK + rows_here] * SCALE
    center_ref[1] = accv[BLOCK : BLOCK + rows_here]
    rim_ref[0, 0] = (acck[0:BLOCK] * SCALE).astype(BF)
    rim_ref[0, 1] = accv[0:BLOCK].astype(BF)
    rim_ref[1, 0] = (acck[BLOCK + rows_here :] * SCALE).astype(BF)
    rim_ref[1, 1] = accv[BLOCK + rows_here :].astype(BF)
    for e in range(per_head):
        s = pick[h * per_head + e]
        d, c = lax.div(s, 2), lax.rem(s, 2)
        rows = pl.ds(e * BLOCK, BLOCK)
        pltpu.make_async_copy(tk.at[slot, rows], outgoing.at[d, c, 0], out_sem.at[slot]).start()
        pltpu.make_async_copy(tv.at[slot, rows], outgoing.at[d, c, 1], out_sem.at[slot]).start()

    @pl.when(h == HEADS_HERE - 1)
    def _():
        drain(1 - slot)
        drain(slot)


def return_kernel(
    outgoing, rim, gpart, returned, rim_back, gother, glast,
    ra, rb, rc, pa, pb, pc, ss, rs, hs, hr, us, ur, ls, lr, bs, br, own_sem,
):
    me = lax.axis_index("seq")
    enter(me)
    after = lax.rem(me + 1, SHARDS)
    before = lax.rem(me + SHARDS - 1, SHARDS)
    own = pltpu.make_async_copy(outgoing.at[0], returned.at[0], own_sem)
    own.start()
    orders = ("yzx", "zyx")
    mine = [pl.ds(first_row(me, order, PIECE), PIECE) for order in orders]
    stages = ((ra, QUART), (rb, 4 * PIECE), (rc, PIECE))
    sums = (pa, pb, pc)

    def reduce_start(g, level, parts=None):
        src = gpart.at[g] if level == 0 else sums[level - 1].at[g]
        dst, rows = stages[level]
        scatter_line(
            me, orders[g][level], src, dst.at[g], rows, us, ur, 12 * g + 4 * level, parts
        )

    def reduce_finish(g, level):
        src = gpart.at[g] if level == 0 else sums[level - 1].at[g]
        dst, rows = stages[level]
        for copy in waits[g][level]:
            copy.wait_recv()
        here = pl.multiple_of(place_of(me, orders[g][level]) * rows, rows)
        total = src[pl.ds(here, rows), :].astype(F32)
        for delta in range(1, 4):
            total = total + dst[g, delta].astype(F32)
        sums[level][g] = total.astype(BF)

    waits = [
        [line_waits(me, ref.at[g], us, ur, 12 * g + 4 * n) for n, (ref, _) in enumerate(stages)]
        for g in range(2)
    ]
    def edge(part, far):
        rows = pl.ds(part * 16, 16)
        for side, target, x in ((0, before, 0), (1, after, 3)):

            @pl.when((place_of(me, "x") == x) == far)
            def _():
                for kv in range(2):
                    remote(
                        rim.at[side, kv, rows], rim_back.at[1 - side, kv, rows],
                        hs.at[2 * side + kv], hr.at[2 * side + kv], target,
                    ).start()

    halos = [
        remote(rim.at[n // 2, n % 2], rim_back.at[n // 2, n % 2], hs.at[n], hr.at[n], me)
        for n in range(4)
    ]
    levels = spread_order(orders[0])
    down = [
        share_waits(me, gother, rows, bs, br, 4 * level) for level, (_, rows) in enumerate(levels)
    ]

    def share(level, parts=None):
        axis, rows = levels[level]
        first = first_row(me, orders[0], rows)
        share_line(me, axis, gother, first, rows, bs, br, 4 * level, parts)

    tree = spread_order(orders[1])

    def on_path(level):
        ok = me >= 0
        for axis, _ in tree[:level]:
            ok = ok & (place_of(me, axis) == 3)
        return ok

    def is_sender(level):
        return on_path(level) & (place_of(me, tree[level][0]) != 3)

    def gather_copy(level, source):
        axis, rows = tree[level]
        ref = glast.at[pl.ds(first_row(me, orders[1], rows), rows)]
        target = me + (3 - place_of(me, axis)) * STEP[axis]
        return remote(ref, ref, ls.at[level], lr.at[4 * level + source], target)

    def gather_send(level):
        @pl.when(is_sender(level))
        def _():
            gather_copy(level, place_of(me, tree[level][0])).start()

    def gather_take(level):
        @pl.when(on_path(level + 1))
        def _():
            for source in range(3):
                gather_copy(level, source).wait_recv()

    for part in range(4):
        for g in range(2):
            reduce_start(g, 0, (part,))
        edge(part, False)
    later = []
    for number, offsets in enumerate(ROUNDS):
        if number >= DEPTH:
            sent_round(me, outgoing, returned, ss, rs, ROUNDS[number - DEPTH])
        for step in later:
            step()
        later = []
        send_round(me, -1, outgoing, returned, ss, rs, offsets)
        if number in RETURN_FAR:
            edge(RETURN_FAR.index(number), True)
        if number == RETURN_AT[0]:
            for g in range(2):
                reduce_finish(g, 0)
                later.append(functools.partial(reduce_start, g, 1))
        if number == RETURN_AT[1]:
            for g in range(2):
                reduce_finish(g, 1)
                later.append(functools.partial(reduce_start, g, 2))
        if number == RETURN_AT[2]:
            for g in range(2):
                reduce_finish(g, 2)
            gother[mine[0], :] = pc[0]

            def pass_on():
                share(0)
                gather_send(0)

            later.append(pass_on)
            glast[mine[1], :] = pc[1]
        if number == RETURN_AT[3]:
            for copy in down[0]:
                copy.wait_recv()
            gather_take(0)
            share(1)
            gather_send(1)
        if number == RETURN_AT[4]:
            for copy in down[1]:
                copy.wait_recv()
            gather_take(1)
            gather_send(2)
        if RETURN_AT[4] <= number < RETURN_AT[4] + 4:
            part = number - RETURN_AT[4]
            share(2, (part,))
            edge(part + 4, False)
    for offsets in ROUNDS[-DEPTH:]:
        sent_round(me, outgoing, returned, ss, rs, offsets)
    for offsets in ROUNDS:
        arrived_round(me, outgoing, returned, ss, rs, offsets)
    for g in range(2):
        for line in waits[g]:
            for copy in line:
                copy.wait_send()
    for level in range(3):
        for copy in down[level]:
            copy.wait_send()
            if level == 2:
                copy.wait_recv()
    for copy in halos:
        copy.wait()

    for level in range(3):

        @pl.when(is_sender(level))
        def _():
            gather_copy(level, 0).wait_send()

    gather_take(2)
    own.wait()


CHUNK = 4


def collect_kernel(
    glob, codes, center, rim, gother, glast, returned, dk_ref, dv_ref, buf, acc, sem, csem
):
    me = lax.axis_index("seq")
    steps = SHARDS // CHUNK

    def fetch(step):
        place = pl.ds(pl.multiple_of(step * CHUNK, CHUNK), CHUNK)
        return pltpu.make_async_copy(returned.at[place], buf.at[place], sem.at[step])

    whole = pltpu.make_async_copy(center, acc, csem)
    whole.start()
    for step in range(steps):
        fetch(step).start()
    whole.wait()
    for kv in range(2):
        acc[kv, 0:BLOCK, :] += rim[0, kv].astype(F32)
        acc[kv, (QB - 1) * BLOCK :, :] += rim[1, kv].astype(F32)

    def add_glob(blk, ref):
        rows = pl.ds(pl.multiple_of(blk * BLOCK, BLOCK), BLOCK)
        for h in range(HEADS_HERE):
            for kv in range(2):
                src = ref[pl.ds((2 * h + kv) * BLOCK, BLOCK), :]
                acc[kv, rows, pl.ds(h * DH, DH)] += src.astype(F32)

    @pl.when(me == LAST)
    def _():
        add_glob(QB - 1, glast)

    other = glob[0] + glob[1] - (SHARDS * QB - 1)

    @pl.when(me == lax.div(other, QB))
    def _():
        add_glob(lax.rem(other, QB), gother)

    def add(code, d, c):
        head = lax.div(code, 4 * QB * RAND)
        blk = lax.rem(code, 4)
        rows = pl.ds(pl.multiple_of(blk * BLOCK, BLOCK), BLOCK)
        cols = pl.ds(pl.multiple_of(head * DH, DH), DH)
        for kv in range(2):
            acc[kv, rows, cols] += buf[d, c, kv].astype(F32)

    def step_body(step, carry):
        fetch(step).wait()
        for place in range(CHUNK):
            d = step * CHUNK + place
            t = moved(me, d)
            low, high = codes[0, t], codes[1, t]

            @pl.when(low < NONE)
            def _():
                add(low, d, 0)

            @pl.when(high > low)
            def _():
                add(high, d, 1)

        return carry

    lax.fori_loop(0, steps, step_body, 0)
    dk_ref[...] = acc[0].astype(BF)
    dv_ref[...] = acc[1].astype(BF)


def smem():
    return pl.BlockSpec(memory_space=pltpu.SMEM)


def vmem():
    return pl.BlockSpec(memory_space=pltpu.VMEM)


def hbm():
    return pl.BlockSpec(memory_space=ANY)


def dma(*shape):
    return pltpu.SemaphoreType.DMA(shape)


def body(queries, keys, values, out_grad, rand_ids, glob_ids):
    place = lax.axis_index("seq")
    group = lax.axis_index("head")
    shape = jax.ShapeDtypeStruct
    ids = lax.dynamic_slice_in_dim(rand_ids, group * HEADS_HERE, HEADS_HERE, 0)
    ids = ids.reshape(HEADS_HERE, SHARDS, QB * RAND)
    own_ids = lax.dynamic_index_in_dim(ids, place, 1, False).reshape(ENTRIES)
    table = ids.transpose(0, 2, 1).reshape(ENTRIES, SHARDS)
    slots = shape((SHARDS, 2, 2, BLOCK, DH), BF)
    grows = shape((GROWS, DH), BF)
    width = HEADS_HERE * DH
    rows_here = QB * BLOCK

    payload, cand_o, cand_l, pick, codes = pl.pallas_call(
        prep_kernel,
        out_shape=(
            slots, grows, grows, shape((ENTRIES,), jnp.int32), shape((2, SHARDS), jnp.int32)
        ),
        in_specs=[smem(), smem(), vmem(), vmem(), vmem()],
        out_specs=(hbm(), hbm(), hbm(), smem(), vmem()),
        scratch_shapes=[
            pltpu.SMEM((SHARDS,), jnp.int32),
            pltpu.SMEM((2, SHARDS), jnp.int32),
            pltpu.SemaphoreType.DMA, dma(2), pltpu.SemaphoreType.DMA,
        ],
        name="prep",
    )(glob_ids, own_ids, table, keys, values)

    recv, halo, gother, glast = pl.pallas_call(
        fetch_kernel,
        out_shape=(slots, shape((2, 2, BLOCK, width), BF), grows, grows),
        in_specs=[smem(), hbm(), hbm(), hbm(), vmem(), vmem()],
        out_specs=(hbm(), hbm(), vmem(), vmem()),
        scratch_shapes=[
            pltpu.VMEM((4, QUART, DH), BF),
            pltpu.VMEM((4, 4 * PIECE, DH), BF),
            pltpu.VMEM((4, PIECE, DH), BF),
            pltpu.VMEM((QUART, DH), BF),
            pltpu.VMEM((4 * PIECE, DH), BF),
            dma(SHARDS), dma(SHARDS), dma(4), dma(4), dma(12), dma(12),
            dma(SHARDS), pltpu.SemaphoreType.DMA, dma(24), dma(24), pltpu.SemaphoreType.DMA,
        ],
        compiler_params=pltpu.CompilerParams(collective_id=0, has_side_effects=True),
        name="fetch",
    )(glob_ids, payload, keys, values, cand_o, cand_l)

    span = 3 * BLOCK
    head_block = pl.BlockSpec((rows_here, DH), lambda h, *_: (0, h))
    side_block = pl.BlockSpec((2, 2, BLOCK, DH), lambda h, *_: (0, 0, 0, h))
    one_block = pl.BlockSpec((1, 2, BLOCK, DH), lambda h, *_: (h, 0, 0, 0))
    glob_block = pl.BlockSpec((2, 1, 2, BLOCK, DH), lambda h, *_: (0, h, 0, 0, 0))
    full = QB * span
    out, dq, center, rim, gpart, outgoing = pl.pallas_call(
        attend_kernel,
        out_shape=(
            shape((rows_here, width), BF),
            shape((rows_here, width), BF),
            shape((2, rows_here, width), F32),
            shape((2, 2, BLOCK, width), BF),
            shape((2, HEADS_HERE, 2, BLOCK, DH), BF),
            slots,
        ),
        grid_spec=pltpu.PrefetchScalarGridSpec(
            num_scalar_prefetch=1,
            grid=(HEADS_HERE,),
            in_specs=[head_block] * 4 + [side_block, one_block, one_block, hbm()],
            out_specs=[
                head_block,
                head_block,
                pl.BlockSpec((2, rows_here, DH), lambda h, *_: (0, 0, h)),
                side_block,
                glob_block,
                hbm(),
            ],
            scratch_shapes=[pltpu.VMEM((2, full, DH), BF)] * 4
            + [pltpu.VMEM((rows_here + 2 * BLOCK, DH), BF)] * 2
            + [pltpu.VMEM((2 * BLOCK, DH), BF)] * 2
            + [pltpu.VMEM((rows_here + 2 * BLOCK, DH), F32)] * 2
            + [pltpu.VMEM((rows_here, 2 * BLOCK), BF)] * 2
            + [dma(2), dma(2)],
        ),
        name="attend",
    )(
        pick, queries, keys, values, out_grad, halo,
        gother.reshape(HEADS_HERE, 2, BLOCK, DH), glast.reshape(HEADS_HERE, 2, BLOCK, DH), recv,
    )

    returned, rim_back, sum_other, sum_last = pl.pallas_call(
        return_kernel,
        out_shape=(slots, shape((2, 2, BLOCK, width), BF), grows, grows),
        in_specs=[hbm(), hbm(), vmem()],
        out_specs=(hbm(), hbm(), vmem(), vmem()),
        scratch_shapes=[
            pltpu.VMEM((2, 4, QUART, DH), BF),
            pltpu.VMEM((2, 4, 4 * PIECE, DH), BF),
            pltpu.VMEM((2, 4, PIECE, DH), BF),
            pltpu.VMEM((2, QUART, DH), BF),
            pltpu.VMEM((2, 4 * PIECE, DH), BF),
            pltpu.VMEM((2, PIECE, DH), BF),
            dma(SHARDS), dma(SHARDS), dma(4), dma(4), dma(24), dma(24),
            dma(3), dma(12), dma(12), dma(12), pltpu.SemaphoreType.DMA,
        ],
        compiler_params=pltpu.CompilerParams(collective_id=1, has_side_effects=True),
        name="return",
    )(outgoing, rim, gpart.reshape(2, GROWS, DH))

    dk, dv = pl.pallas_call(
        collect_kernel,
        out_shape=(shape((rows_here, width), BF), shape((rows_here, width), BF)),
        in_specs=[smem(), smem(), hbm(), vmem(), vmem(), vmem(), hbm()],
        out_specs=(vmem(), vmem()),
        scratch_shapes=[
            pltpu.VMEM((SHARDS, 2, 2, BLOCK, DH), BF),
            pltpu.VMEM((2, rows_here, width), F32),
            dma(SHARDS // CHUNK),
            pltpu.SemaphoreType.DMA,
        ],
        name="collect",
    )(glob_ids, codes, center, rim_back, sum_other, sum_last, returned)
    return out, dq, dk, dv


def solution(mesh):
    rows = P("seq", "head")
    return jax.shard_map(
        body,
        mesh=mesh,
        in_specs=(rows, rows, rows, rows, P(), P()),
        out_specs=(rows, rows, rows, rows),
        check_vma=False,
    )
```
